32 devices in a mesh: dp: 8 (over z, x), ctx: 4 (over y, core).
Axes of the slice: x: 2, y: 2, z: 4, core: 2. Of those that a mesh axis runs over, the one named last changes fastest.
Arguments:
- hidden_in: bfloat16 [32, 1024, 960], P('dp', 'ctx'), may hold values from -41 to 41
- norm_gains: bfloat16 [1920], P(('dp', 'ctx')), may hold values from 0.099609375 to 1.8984375
- w_query: bfloat16 [960, 960], P('ctx', 'dp'), may hold values from -0.1875 to 0.1875
- w_key: bfloat16 [960, 320], P('ctx', 'dp'), may hold values from -0.1875 to 0.1875
- w_value: bfloat16 [960, 320], P('ctx', 'dp'), may hold values from -0.1875 to 0.1875
- w_out: bfloat16 [960, 960], P('ctx', 'dp'), may hold values from -1.5 to 1.5
- w_gate: bfloat16 [960, 2560], P('ctx', 'dp'), may hold values from -0.1875 to 0.1875
- w_up: bfloat16 [960, 2560], P('ctx', 'dp'), may hold values from -0.1875 to 0.1875
- w_down: bfloat16 [2560, 960], P('ctx', 'dp'), may hold values from -0.125 to 0.125
- cotangent: bfloat16 [32, 1024, 960], P('dp', 'ctx'), may hold values from -6 to 6
Outputs:
- hidden_out: bfloat16 [32, 1024, 960], P('dp', 'ctx')
- hidden_grad: bfloat16 [32, 1024, 960], P('dp', 'ctx')
- gains_grad: float32 [1920], P(('dp', 'ctx'))
- query_grad: float32 [960, 960], P('ctx', 'dp')
- key_grad: float32 [960, 320], P('ctx', 'dp')
- value_grad: float32 [960, 320], P('ctx', 'dp')
- out_grad: float32 [960, 960], P('ctx', 'dp')
- gate_grad: float32 [960, 2560], P('ctx', 'dp')
- up_grad: float32 [960, 2560], P('ctx', 'dp')
- down_grad: float32 [2560, 960], P('ctx', 'dp')
The draws below stay inside these ranges and needn't reach their ends.
All inputs are finite; a program needn't handle non-finite values.
Results may differ from the reference program's by a relative error of at most 0.014.
Values may be sent and summed in bfloat16 or wider, within the bound.
No kernel may reach another device: no remote copies, remote signals or barrier semaphores. Data moves between devices by JAX's collectives and lax.ppermute only.
A program may use at most 640 MiB of HBM per device.

```python
import math
import jax
import jax.numpy as jnp
from jax import lax

D = 960
QH = 15
KVH = 5
HD = 64
FF = 2560
SEQ_DEV = 4
QD = 960
KVD = 320
LEN = 1024
SEQS = 32
TOKENS = 32768
N_DP = 8


def draw_hidden_in(key, part):
    row_scale = jnp.exp(jax.random.uniform(jax.random.fold_in(key, 11), (SEQS, LEN, 1), jnp.float32, math.log(0.3), math.log(3.0)))
    col_scale = jnp.exp(jax.random.uniform(jax.random.fold_in(key, 12), (D,), jnp.float32, math.log(0.3), math.log(3.0)))
    base_part = jax.random.truncated_normal(jax.random.fold_in(key, 14), -4.0, 4.0, (SEQS, LEN, D), jnp.float32)
    return (base_part * row_scale * col_scale[None, None, :]).astype(jnp.bfloat16)


def levels(key, dims, split, smallest, largest):
    def one(axis_at, parts):
        heights = jax.random.uniform(jax.random.fold_in(jax.random.fold_in(key, 6), axis_at), (parts,), jnp.float32, smallest / len(split), largest / len(split))
        return jnp.repeat(jnp.exp(heights), dims[axis_at] // parts).reshape((-1,) + (1,) * (len(dims) - axis_at - 1))

    factor_of = one(*split[0])
    for cut in split[1:]:
        factor_of = factor_of * one(*cut)
    return factor_of


def normal_values(own_key, dims, scale, most, cuts=(), dtype=jnp.bfloat16):
    entries = scale * jax.random.normal(own_key, dims, jnp.float32)
    if cuts:
        entries = entries * levels(own_key, dims, cuts, -0.22, 0.18)
    return jnp.clip(entries, -most, most).astype(dtype)


def setup_inputs(seed: int = 0) -> dict:
    arg_keys = jax.random.split(jax.random.key(seed), 11)
    hidden_in = draw_hidden_in(jax.random.fold_in(arg_keys[10], 71), 0)
    norm_gains = jnp.clip(1.0 + 0.18 * jax.random.normal(arg_keys[1], (2 * D,), jnp.float32), 0.099609375, 1.8984375).astype(jnp.bfloat16)
    w_query = normal_values(arg_keys[2], (D, QD), D ** -0.5, 0.1875, ((0, 4), (1, 8)))
    w_key = normal_values(arg_keys[3], (D, KVD), D ** -0.5, 0.1875, ((0, 4), (1, 8)))
    w_value = normal_values(arg_keys[4], (D, KVD), D ** -0.5, 0.1875, ((0, 4), (1, 8)))
    w_out = normal_values(arg_keys[5], (QD, D), (max(QD * 16 // LEN, 1)) ** -0.5, 1.5, ((0, 4), (1, 8)))
    w_gate = normal_values(arg_keys[6], (D, FF), D ** -0.5, 0.1875, ((0, 4), (1, 8)))
    w_up = normal_values(arg_keys[7], (D, FF), D ** -0.5, 0.1875, ((0, 4), (1, 8)))
    w_down = normal_values(arg_keys[8], (FF, D), FF ** -0.5, 0.125, ((0, 4), (1, 8)))
    cotangent = normal_values(arg_keys[9], (SEQS, LEN, D), 1.0, 6.0, ((0, 8), (1, 4)))
    return {"hidden_in": hidden_in, "norm_gains": norm_gains, "w_query": w_query, "w_key": w_key, "w_value": w_value, "w_out": w_out, "w_gate": w_gate, "w_up": w_up, "w_down": w_down, "cotangent": cotangent}


epsilon = 1e-05
rope_base = 100000.0
masked_score = -1e+30

@jax.custom_vjp
def low(v):
    return lax.optimization_barrier(v.astype(jnp.bfloat16)).astype(jnp.float32)

@jax.custom_vjp
def low_back(v):
    return v

def low_keep(v):
    return (low(v), None)

def low_pass(kept, grad):
    return (grad,)

def back_keep(v):
    return (v, None)

def back_low(kept, grad):
    return (low(grad),)
low.defvjp(low_keep, low_pass)
low_back.defvjp(back_keep, back_low)

def matmul(leading, trailing):
    return jnp.dot(leading, trailing, precision=lax.Precision.HIGHEST, preferred_element_type=jnp.float32)

def rope_tables(positions, head_size):
    half_size = head_size // 2
    frequencies = jnp.exp(-(jnp.arange(half_size).astype(jnp.float32) * (2.0 / head_size)) * math.log(rope_base))
    angles = positions[:, None] * frequencies[None, :]
    angles = jnp.concatenate([angles, angles], axis=-1)
    return (jnp.cos(angles), jnp.sin(angles))

def rotate(values, cos_table, sin_table):
    half_size = values.shape[-1] // 2
    turned = jnp.concatenate([-values[..., half_size:], values[..., :half_size]], axis=-1)
    return values * cos_table[:, None, :] + turned * sin_table[:, None, :]

def rms_scale(values, gain_row):
    return values * lax.rsqrt(lax.optimization_barrier(jnp.mean(values * values, axis=-1, keepdims=True)) + epsilon) * gain_row

def attend_one(triple):
    query_set, key_set, value_set = triple
    seq_length = query_set.shape[0]
    raw_scores = jnp.einsum('qhgd,khd->hgqk', query_set, key_set, precision=lax.Precision.HIGHEST) * HD ** (-0.5)
    ordered = jnp.arange(seq_length)
    causal = ordered[:, None] >= ordered[None, :]
    scores = jnp.where(causal, low_back(raw_scores), masked_score)
    weights = low(jax.nn.softmax(scores, axis=-1))
    return jnp.einsum('hgqk,khd->qhgd', weights, value_set, precision=lax.Precision.HIGHEST)

def layer(inputs, norm_gains, w_query, w_key, w_value, w_out, w_gate, w_up, w_down):
    seq_count, seq_length = (inputs.shape[0], inputs.shape[1])
    per_group = QH // KVH
    cos_table, sin_table = rope_tables(jnp.arange(seq_length).astype(jnp.float32), HD)
    normed = low(rms_scale(inputs, norm_gains[:D]))
    queries = low_back(matmul(normed, w_query)).reshape(seq_count, seq_length, QH, HD)
    key_proj = low_back(matmul(normed, w_key)).reshape(seq_count, seq_length, KVH, HD)
    value_proj = low(low_back(matmul(normed, w_value))).reshape(seq_count, seq_length, KVH, HD)
    turned_query = low(rotate(queries, cos_table, sin_table)).reshape(seq_count, seq_length, KVH, per_group, HD)
    turned_key = low(rotate(key_proj, cos_table, sin_table))
    attended = lax.map(jax.checkpoint(attend_one), (turned_query, turned_key, value_proj))
    mixed_heads = low(low_back(attended.reshape(seq_count, seq_length, QH * HD)))
    middle = inputs + low_back(matmul(mixed_heads, w_out))
    normed_two = low(rms_scale(middle, norm_gains[D:]))
    gate_pre = low_back(matmul(normed_two, w_gate))
    up_pre = low_back(matmul(normed_two, w_up))
    product = low(jax.nn.silu(gate_pre) * up_pre)
    return middle + low_back(matmul(product, w_down))

def reference(hidden_in, norm_gains, w_query, w_key, w_value, w_out, w_gate, w_up, w_down, cotangent):
    weights = (norm_gains.astype(jnp.float32), w_query.astype(jnp.float32), w_key.astype(jnp.float32), w_value.astype(jnp.float32), w_out.astype(jnp.float32), w_gate.astype(jnp.float32), w_up.astype(jnp.float32), w_down.astype(jnp.float32))
    inputs = hidden_in.astype(jnp.float32).reshape(N_DP, SEQ_DEV, LEN, D)
    seeds = cotangent.astype(jnp.float32).reshape(N_DP, SEQ_DEV, LEN, D)

    def advance(running, block_pair):
        block_in, block_seed = block_pair
        result, pullback = jax.vjp(layer, block_in, *weights)
        gradients = pullback(block_seed)
        running = tuple((partial_sum + gradient for partial_sum, gradient in zip(running, gradients[1:])))
        return (running, (result.astype(jnp.bfloat16), gradients[0].astype(jnp.bfloat16)))
    starts = tuple((jnp.zeros(weight.shape, jnp.float32) for weight in weights))
    sums, (outputs, input_grads) = lax.scan(advance, starts, (inputs, seeds))
    factor = 1.0 / math.sqrt(TOKENS)
    return (outputs.reshape(SEQS, LEN, D), input_grads.reshape(SEQS, LEN, D), sums[0] * factor, sums[1] * factor, sums[2] * factor, sums[3] * factor, sums[4] * factor, sums[5] * factor, sums[6] * factor, sums[7] * factor)
```

```python
import functools
import math

import jax
import jax.numpy as jnp
from jax import lax
from jax.experimental import pallas as pl
from jax.experimental.pallas import tpu as pltpu
from jax.sharding import PartitionSpec as P


QH = 15
KVH = 5
HD = 64


epsilon = 1e-05
rope_base = 100000.0
masked_score = -1e30
contract_last = (((1,), (1,)), ((), ()))
contract_first = (((0,), (0,)), ((), ()))


def rope_tables(positions, head_size):
    half_size = head_size // 2
    frequencies = jnp.exp(
        -(jnp.arange(half_size).astype(jnp.float32) * (2.0 / head_size)) * math.log(rope_base)
    )
    angles = positions[:, None] * frequencies[None, :]
    angles = jnp.concatenate([angles, angles], axis=-1)
    return (jnp.cos(angles), jnp.sin(angles))


def rotate(values, cos_table, sin_table):
    half_size = values.shape[-1] // 2
    turned = jnp.concatenate([-values[..., half_size:], values[..., :half_size]], axis=-1)
    return values * cos_table[:, None, :] + turned * sin_table[:, None, :]


def unrotate(grad_turned, cos_table, sin_table):
    _, pullback = jax.vjp(lambda values: rotate(values, cos_table, sin_table), grad_turned)
    return pullback(grad_turned)[0]


def rms_scale(values, gain_row):
    return (
        values * lax.rsqrt(jnp.mean(values * values, axis=-1, keepdims=True) + epsilon) * gain_row
    )


def local(hidden_in, norm_gains, w_query, w_key, w_value, w_out, w_gate, w_up, w_down, cotangent):
    seqs_here, seg_len, model_width = hidden_in.shape
    ctx_size = lax.axis_size("ctx")
    dp_size = lax.axis_size("dp")
    full_len = seg_len * ctx_size
    rows_here = seqs_here * seg_len
    per_group = QH // KVH
    score_scale = HD ** (-0.5)
    row_parts = (
        lax.all_gather(w_query, "ctx", axis=0, tiled=True),
        lax.all_gather(w_key, "ctx", axis=0, tiled=True),
        lax.all_gather(w_value, "ctx", axis=0, tiled=True),
        lax.all_gather(w_out, "ctx", axis=0, tiled=True),
        lax.all_gather(w_gate, "ctx", axis=0, tiled=True),
        lax.all_gather(w_up, "ctx", axis=0, tiled=True),
        lax.all_gather(w_down, "ctx", axis=0, tiled=True),
        lax.all_gather(norm_gains.reshape(-1, 1), "ctx", axis=0, tiled=True),
    )
    gathered = (
        lax.all_gather(row_parts[0], "dp", axis=1, tiled=True),
        lax.all_gather(row_parts[1], "dp", axis=1, tiled=True),
        lax.all_gather(row_parts[2], "dp", axis=1, tiled=True),
        lax.all_gather(row_parts[3], "dp", axis=1, tiled=True),
        lax.all_gather(row_parts[4], "dp", axis=1, tiled=True),
        lax.all_gather(row_parts[5], "dp", axis=1, tiled=True),
        lax.all_gather(row_parts[6], "dp", axis=1, tiled=True),
        lax.all_gather(row_parts[7].reshape(1, -1), "dp", axis=1, tiled=True),
    )
    first_pos = lax.axis_index("ctx") * seg_len + jnp.arange(seg_len)
    cos_table, sin_table = rope_tables(first_pos.astype(jnp.float32), HD)
    row_pos = jnp.tile(first_pos, per_group)
    causal_mask = jnp.arange(full_len)[None, :] <= row_pos[:, None]

    def group_queries(tensor):
        return (
            tensor.reshape(seqs_here, seg_len, KVH, per_group, HD)
            .transpose(0, 2, 3, 1, 4)
            .reshape(seqs_here * KVH, per_group * seg_len, HD)
        )

    def ungroup_queries(tensor):
        return (
            tensor.reshape(seqs_here, KVH, per_group, seg_len, HD)
            .transpose(0, 3, 1, 2, 4)
            .reshape(rows_here, QH * HD)
        )

    def group_keys(tensor):
        return (
            tensor.reshape(seqs_here, full_len, KVH, HD)
            .transpose(0, 2, 1, 3)
            .reshape(seqs_here * KVH, full_len, HD)
        )

    def ungroup_keys(tensor):
        return (
            tensor.reshape(seqs_here, KVH, full_len, HD)
            .transpose(0, 2, 1, 3)
            .reshape(seqs_here, full_len, KVH * HD)
        )

    def block_scores(query_block, key_block):
        raw_scores = (
            lax.dot_general(
                query_block, key_block, contract_last, preferred_element_type=jnp.float32
            )
            * score_scale
        )
        return jnp.where(causal_mask, raw_scores, masked_score)

    def attend_forward(triple):
        query_block, key_block, value_block = triple
        scores = block_scores(query_block, key_block)
        row_top = jnp.max(scores, axis=-1, keepdims=True)
        exponents = jnp.exp(scores - row_top)
        totals = jnp.sum(exponents, axis=-1, keepdims=True)
        attn_weights = exponents / totals
        attended = jnp.dot(
            attn_weights.astype(jnp.bfloat16), value_block, preferred_element_type=jnp.float32
        )
        return (attended, (row_top + jnp.log(totals))[:, 0])

    gains_full = gathered[7].reshape(-1).astype(jnp.float32)
    inputs_f32 = hidden_in.reshape(rows_here, model_width).astype(jnp.float32)
    normed = rms_scale(inputs_f32, gains_full[:model_width]).astype(jnp.bfloat16)
    queries = jnp.dot(normed, gathered[0], preferred_element_type=jnp.float32).reshape(
        seqs_here, seg_len, QH, HD
    )
    key_proj = jnp.dot(normed, gathered[1], preferred_element_type=jnp.float32).reshape(
        seqs_here, seg_len, KVH, HD
    )
    value_proj = (
        jnp.dot(normed, gathered[2], preferred_element_type=jnp.float32)
        .astype(jnp.bfloat16)
        .reshape(seqs_here, seg_len, KVH * HD)
    )
    turned_query = rotate(queries, cos_table, sin_table).astype(jnp.bfloat16)
    turned_key = (
        rotate(key_proj, cos_table, sin_table)
        .astype(jnp.bfloat16)
        .reshape(seqs_here, seg_len, KVH * HD)
    )
    key_sets = (
        lax.all_gather(turned_key, "ctx", axis=1, tiled=True),
        lax.all_gather(value_proj, "ctx", axis=1, tiled=True),
    )
    grouped_query = group_queries(turned_query)
    attended, log_totals = lax.map(
        attend_forward, (grouped_query, group_keys(key_sets[0]), group_keys(key_sets[1]))
    )
    mixed_heads = ungroup_queries(attended).astype(jnp.bfloat16)
    middle = inputs_f32 + jnp.dot(mixed_heads, gathered[3], preferred_element_type=jnp.float32)
    normed_two = rms_scale(middle, gains_full[model_width:]).astype(jnp.bfloat16)
    gate_pre = jnp.dot(normed_two, gathered[4], preferred_element_type=jnp.float32)
    up_pre = jnp.dot(normed_two, gathered[5], preferred_element_type=jnp.float32)
    product = (jax.nn.silu(gate_pre) * up_pre).astype(jnp.bfloat16)
    result = middle + jnp.dot(product, gathered[6], preferred_element_type=jnp.float32)
    hidden_out = result.astype(jnp.bfloat16).reshape(seqs_here, seg_len, model_width)
    rows_again = (
        lax.all_gather(w_query, "ctx", axis=0, tiled=True),
        lax.all_gather(w_key, "ctx", axis=0, tiled=True),
        lax.all_gather(w_value, "ctx", axis=0, tiled=True),
        lax.all_gather(w_out, "ctx", axis=0, tiled=True),
        lax.all_gather(w_gate, "ctx", axis=0, tiled=True),
        lax.all_gather(w_up, "ctx", axis=0, tiled=True),
        lax.all_gather(w_down, "ctx", axis=0, tiled=True),
        lax.all_gather(norm_gains.reshape(-1, 1), "ctx", axis=0, tiled=True),
    )
    refetched = (
        lax.all_gather(rows_again[0], "dp", axis=1, tiled=True),
        lax.all_gather(rows_again[1], "dp", axis=1, tiled=True),
        lax.all_gather(rows_again[2], "dp", axis=1, tiled=True),
        lax.all_gather(rows_again[3], "dp", axis=1, tiled=True),
        lax.all_gather(rows_again[4], "dp", axis=1, tiled=True),
        lax.all_gather(rows_again[5], "dp", axis=1, tiled=True),
        lax.all_gather(rows_again[6], "dp", axis=1, tiled=True),
        lax.all_gather(rows_again[7].reshape(1, -1), "dp", axis=1, tiled=True),
    )
    keys_again = (
        lax.all_gather(turned_key, "ctx", axis=1, tiled=True),
        lax.all_gather(value_proj, "ctx", axis=1, tiled=True),
    )
    gains_back = refetched[7].reshape(-1).astype(jnp.float32)
    seed_low = cotangent.reshape(rows_here, model_width)
    seed_high = seed_low.astype(jnp.float32)
    down_part = lax.dot_general(
        product, seed_low, contract_first, preferred_element_type=jnp.float32
    )
    grad_product = lax.dot_general(
        seed_low, refetched[6], contract_last, preferred_element_type=jnp.float32
    )
    _, gate_pull = jax.vjp(
        lambda gate_in, up_in: jax.nn.silu(gate_in) * up_in, gate_pre, up_pre
    )
    grad_gate, grad_up = gate_pull(grad_product)
    grad_gate = grad_gate.astype(jnp.bfloat16)
    grad_up = grad_up.astype(jnp.bfloat16)
    gate_part = lax.dot_general(
        normed_two, grad_gate, contract_first, preferred_element_type=jnp.float32
    )
    up_part = lax.dot_general(
        normed_two, grad_up, contract_first, preferred_element_type=jnp.float32
    )
    grad_normed_two = lax.dot_general(
        grad_gate, refetched[4], contract_last, preferred_element_type=jnp.float32
    ) + lax.dot_general(grad_up, refetched[5], contract_last, preferred_element_type=jnp.float32)
    _, second_pull = jax.vjp(rms_scale, middle, gains_back[model_width:])
    grad_middle_norm, gain_two_part = second_pull(grad_normed_two)
    grad_middle = seed_high + grad_middle_norm
    grad_branch = grad_middle.astype(jnp.bfloat16)
    out_part = lax.dot_general(
        mixed_heads, grad_branch, contract_first, preferred_element_type=jnp.float32
    )
    grad_mixed = lax.dot_general(
        grad_branch, refetched[3], contract_last, preferred_element_type=jnp.float32
    ).astype(jnp.bfloat16)

    def attend_backward(bundle):
        query_block, key_block, value_block, log_total, grad_block = bundle
        scores = block_scores(query_block, key_block)
        attn_weights = jnp.exp(scores - log_total[:, None])
        grad_weights = lax.dot_general(
            grad_block, value_block, contract_last, preferred_element_type=jnp.float32
        )
        grad_values = lax.dot_general(
            attn_weights.astype(jnp.bfloat16),
            grad_block,
            contract_first,
            preferred_element_type=jnp.float32,
        )
        grad_scores = (
            attn_weights
            * (grad_weights - jnp.sum(attn_weights * grad_weights, axis=-1, keepdims=True))
        ).astype(jnp.bfloat16)
        grad_queries = (
            jnp.dot(grad_scores, key_block, preferred_element_type=jnp.float32) * score_scale
        )
        grad_keys = (
            lax.dot_general(
                grad_scores, query_block, contract_first, preferred_element_type=jnp.float32
            )
            * score_scale
        )
        return (grad_queries, grad_keys, grad_values)

    grad_grouped = group_queries(grad_mixed.reshape(seqs_here, seg_len, QH, HD))
    query_blocks, key_blocks, value_blocks = lax.map(
        attend_backward,
        (
            grouped_query,
            group_keys(keys_again[0]),
            group_keys(keys_again[1]),
            log_totals,
            grad_grouped,
        ),
    )
    key_sums = (
        lax.psum_scatter(ungroup_keys(key_blocks), "ctx", scatter_dimension=1, tiled=True),
        lax.psum_scatter(ungroup_keys(value_blocks), "ctx", scatter_dimension=1, tiled=True),
    )
    grad_query = (
        unrotate(
            ungroup_queries(query_blocks).reshape(seqs_here, seg_len, QH, HD), cos_table, sin_table
        )
        .astype(jnp.bfloat16)
        .reshape(rows_here, QH * HD)
    )
    grad_key = (
        unrotate(key_sums[0].reshape(seqs_here, seg_len, KVH, HD), cos_table, sin_table)
        .astype(jnp.bfloat16)
        .reshape(rows_here, KVH * HD)
    )
    grad_value = key_sums[1].astype(jnp.bfloat16).reshape(rows_here, KVH * HD)
    query_part = lax.dot_general(
        normed, grad_query, contract_first, preferred_element_type=jnp.float32
    )
    key_part = lax.dot_general(normed, grad_key, contract_first, preferred_element_type=jnp.float32)
    value_part = lax.dot_general(
        normed, grad_value, contract_first, preferred_element_type=jnp.float32
    )
    grad_normed = (
        lax.dot_general(grad_query, refetched[0], contract_last, preferred_element_type=jnp.float32)
        + lax.dot_general(grad_key, refetched[1], contract_last, preferred_element_type=jnp.float32)
        + lax.dot_general(
            grad_value, refetched[2], contract_last, preferred_element_type=jnp.float32
        )
    )
    _, first_pull = jax.vjp(rms_scale, inputs_f32, gains_back[:model_width])
    grad_inputs_norm, gain_one_part = first_pull(grad_normed)
    hidden_grad = (
        (grad_middle + grad_inputs_norm)
        .astype(jnp.bfloat16)
        .reshape(seqs_here, seg_len, model_width)
    )
    gain_part = jnp.concatenate([gain_one_part, gain_two_part])
    col_sums = (
        lax.psum_scatter(query_part, "dp", scatter_dimension=1, tiled=True),
        lax.psum_scatter(key_part, "dp", scatter_dimension=1, tiled=True),
        lax.psum_scatter(value_part, "dp", scatter_dimension=1, tiled=True),
        lax.psum_scatter(out_part, "dp", scatter_dimension=1, tiled=True),
        lax.psum_scatter(gate_part, "dp", scatter_dimension=1, tiled=True),
        lax.psum_scatter(up_part, "dp", scatter_dimension=1, tiled=True),
        lax.psum_scatter(down_part, "dp", scatter_dimension=1, tiled=True),
        lax.psum_scatter(gain_part.reshape(1, -1), "dp", scatter_dimension=1, tiled=True),
    )
    owned = (
        lax.psum_scatter(col_sums[0], "ctx", scatter_dimension=0, tiled=True),
        lax.psum_scatter(col_sums[1], "ctx", scatter_dimension=0, tiled=True),
        lax.psum_scatter(col_sums[2], "ctx", scatter_dimension=0, tiled=True),
        lax.psum_scatter(col_sums[3], "ctx", scatter_dimension=0, tiled=True),
        lax.psum_scatter(col_sums[4], "ctx", scatter_dimension=0, tiled=True),
        lax.psum_scatter(col_sums[5], "ctx", scatter_dimension=0, tiled=True),
        lax.psum_scatter(col_sums[6], "ctx", scatter_dimension=0, tiled=True),
        lax.psum_scatter(col_sums[7].reshape(-1, 1), "ctx", scatter_dimension=0, tiled=True),
    )
    factor = 1.0 / math.sqrt(dp_size * seqs_here * full_len)
    return (
        hidden_out,
        hidden_grad,
        owned[7].reshape(-1) * factor,
        owned[0] * factor,
        owned[1] * factor,
        owned[2] * factor,
        owned[3] * factor,
        owned[4] * factor,
        owned[5] * factor,
        owned[6] * factor,
    )


BF=jnp.bfloat16; F32=jnp.float32
T=1024; D=960; DP=1024
NT=(((1,),(1,)),((),())); NN=(((1,),(0,)),((),())); TN=(((0,),(0,)),((),()))
def dot(a,b,dn=NN): return lax.dot_general(a,b,dn,preferred_element_type=F32)
ANY=pl.BlockSpec(memory_space=pl.ANY)
SMEM=pl.BlockSpec(memory_space=pltpu.SMEM)
def flip(a,b): return lax.bitwise_xor(a,b)
def const(shape): return pl.BlockSpec(shape,lambda *g:(0,)*len(shape))
def params(): return pltpu.CompilerParams(vmem_limit_bytes=60<<20)
def cost(us): return pl.CostEstimate(flops=int(us*9e8),bytes_accessed=int(us*2e6),transcendentals=0)
def sds(shape,dt): return jax.ShapeDtypeStruct(shape,dt)

def pieces_of(idx, order):
    for p in range(4):
        for f in range(2):
            dx,dy=(p%2,f) if order=="yx" else (f,p%2)
            x=flip(idx[1],dx); ctx=flip(idx[2],dy)*2+flip(idx[3],p//2)
            yield p,f,x,ctx,flip(idx[2],dy)

def load_rows(idx, pieces, dst, sem, groups):
    for z in groups:
        dz=lax.rem(z-idx[0]+4,4)
        for p,f,x,ctx,_ in pieces_of(idx,"yx"):
            pltpu.make_async_copy(pieces[p].at[f,dz], dst.at[2*z+x,pl.ds(pl.multiple_of(ctx*240,16),240)], sem.at[z//2]).start()

def wait_rows(dst, sem, j):
    half=dst.at[pl.ds(4*j,4),pl.ds(0,960)]
    pltpu.make_async_copy(half,half,sem.at[j]).wait()

def load_cols(idx, pieces, dst, sem):
    for p,f,x,ctx,y in pieces_of(idx,"xy"):
        for dz in range(4):
            for t in range(dst.shape[2]//128):
                pltpu.make_async_copy(pieces[p].at[f,dz,:,pl.ds(128*t,128)], dst.at[ctx,lax.rem(idx[0]+dz,4)*2+x,pl.ds(128*t,128)], sem.at[y]).start()

def wait_cols(dst, sem, j):
    half=dst.at[pl.ds(2*j,2)]
    pltpu.make_async_copy(half,half,sem.at[j]).wait()

def ffn_fwd_kernel(S, last, idx, n2, mid, *refs):
    gp=refs[:4]; dp_=refs[4:8]
    out, h_ref, wd_ref, gu_s, d_s, acc, sem = refs[8:]
    j=pl.program_id(0); i=pl.program_id(1)
    @pl.when((j==0)&(i==0))
    def _():
        load_rows(idx,gp,gu_s,sem.at[0],(0,1))
        load_cols(idx,dp_,d_s,sem.at[1])
        load_rows(idx,gp,gu_s,sem.at[0],(2,3))
    @pl.when(i==0)
    def _():
        wait_rows(gu_s,sem.at[0],j); wait_cols(d_s,sem.at[1],j)
        for k in range(4): gu_s[4*j+k,960:1024,:]=jnp.zeros((64,2*S),BF)
        for b in range(2):
            wd_ref[0,b*2*S:(b+1)*2*S,:]=jnp.concatenate([d_s[2*j+b,k][:,:120] for k in range(8)]+[jnp.zeros((2*S,64),BF)],axis=-1)
    rows=pl.ds(pl.multiple_of(i*256,256),256)
    xb=n2[rows,:]
    acts=[]
    for q in range(2):
        w=jnp.concatenate([gu_s[4*j+2*q],gu_s[4*j+2*q+1]],axis=-1)
        h=dot(xb,w)
        h_ref[0,:,q*4*S:(q+1)*4*S]=h.astype(BF)
        for b in range(2):
            g=h[:,b*2*S:b*2*S+S]; u=h[:,b*2*S+S:b*2*S+2*S]
            acts.append((g/(1+jnp.exp(-g))*u).astype(BF))
    act=jnp.concatenate(acts,axis=-1)
    o=dot(act,wd_ref[0])
    @pl.when(j==0)
    def _(): acc[rows,:]=o+mid[rows,:]
    @pl.when(j==1)
    def _():
        r=acc[rows,:]+o
        if last: out[0,0]=r.T[:D,:].astype(BF)
        else: out[...]=r

def ffn_fwd(idx, n2, mid, gp, dp_, last):
    S=gp[0].shape[3]//2
    full=pl.BlockSpec((T,DP),lambda j,i,idx:(0,0))
    if last: ospec=pl.BlockSpec((1,1,D,256),lambda j,i,idx:(flip((i*j)%2,idx[3]),flip((i*j)//2,idx[2]),0,0))
    else: ospec=pl.BlockSpec((256,DP),lambda j,i,idx:(i*j,0))
    return pl.pallas_call(functools.partial(ffn_fwd_kernel,S,last), grid_spec=pltpu.PrefetchScalarGridSpec(num_scalar_prefetch=1,grid=(2,4),
        in_specs=[full,full]+[ANY]*8,
        out_specs=[ospec, pl.BlockSpec((1,256,8*S),lambda j,i,idx:(j,i,0)), pl.BlockSpec((1,4*S,DP),lambda j,i,idx:(j,0,0))],
        scratch_shapes=[pltpu.VMEM((8,DP,2*S),BF),pltpu.VMEM((4,8,2*S,128),BF),pltpu.VMEM((T,DP),F32),pltpu.SemaphoreType.DMA((2,2))]),
        out_shape=[sds((2,2,D,256),BF) if last else sds((T,DP),F32),sds((2,T,8*S),BF),sds((2,4*S,DP),BF)],
        compiler_params=params(), cost_estimate=cost(20), name="ffn_fwd")(idx,n2,mid,*gp,*dp_)

def slot_of(idx, dpi, ctx):
    z=dpi//2; x=dpi%2; y=ctx//2; c=ctx%2
    return flip(c,idx[3]), flip(x,idx[1]), flip(y,idx[2]), lax.rem(z-idx[0]+4,4)

def put(idx, src, keep, send, sem, yx, dpi, ctx, *at):
    c,x,y,z=slot_of(idx,dpi,ctx)
    if yx: x,y=y,x
    @pl.when(c==0)
    def _(): pltpu.make_async_copy(src,keep.at[(x,y,z)+at],sem).start()
    @pl.when(c==1)
    def _(): pltpu.make_async_copy(src,send.at[(x,y,z)+at],sem).start()

def ffn_bwd_kernel(S, idx, cb, n2, h, wd, dn2in, *refs):
    gp=refs[:4]
    dn2, gk, gs, gu_s, dh_s, act_s, dw_s, dd_s, sem, osem = refs[4:]
    q=pl.program_id(0)
    nq=4*S
    @pl.when(q==0)
    def _(): load_rows(idx,gp,gu_s,sem,(0,1,2,3))
    wait_rows(gu_s,sem,q)
    for k in range(4): gu_s[4*q+k,960:1024,:]=jnp.zeros((64,2*S),BF)
    w=jnp.concatenate([gu_s[4*q+k] for k in range(4)],axis=-1)
    wdq=wd[0]
    def rows_step(i,_):
        rows=pl.ds(pl.multiple_of(i*256,256),256)
        dact=dot(cb[rows,:],wdq,NT)
        parts=[];acts=[]
        for b in range(4):
            g=h[0,rows,b*2*S:b*2*S+S].astype(F32); u=h[0,rows,b*2*S+S:b*2*S+2*S].astype(F32)
            da=dact[:,b*S:(b+1)*S]
            sg=1/(1+jnp.exp(-g)); sl=g*sg
            acts.append((sl*u).astype(BF))
            parts.append((da*u*(sg+sl*(1-sg))).astype(BF)); parts.append((da*sl).astype(BF))
        dh=jnp.concatenate(parts,axis=-1)
        dh_s[rows,:]=dh; act_s[rows,:]=jnp.concatenate(acts,axis=-1)
        t=dot(dh,w,NT)
        dn2[rows,:]=jnp.where(q==0,dn2in[rows,:],dn2[rows,:])+t
        return 0
    lax.fori_loop(0,4,rows_step,0)
    @pl.when(q==1)
    def _():
        pltpu.make_async_copy(dw_s.at[pl.ds(0,960)],dw_s.at[pl.ds(0,960)],osem.at[0]).wait()
        pltpu.make_async_copy(dd_s,dd_s,osem.at[1]).wait()
    def dw_step(m,_):
        cols=pl.ds(pl.multiple_of(m*256,256),256)
        dw_s[cols,:]=dot(n2[:,cols],dh_s[...],TN).astype(BF)
        return 0
    lax.fori_loop(0,4,dw_step,0)
    for b in range(4):
        for ctx in range(4):
            put(idx,dw_s.at[pl.ds(ctx*240,240),pl.ds(b*2*S,2*S)],gk,gs,osem.at[0],False,4*q+b,ctx,pl.ds(0,240))
    for m in range(nq//256):
        r=dot(act_s[:,m*256:(m+1)*256],cb[...],TN)
        for k in range(8):
            dd_s[k,m*256:(m+1)*256,:]=jnp.concatenate([r[:,k*120:(k+1)*120],jnp.zeros((256,8),F32)],axis=-1).astype(BF)
    for k in range(8):
        for cc in range(2):
            for t in range(2*S//128):
                put(idx,dd_s.at[k,pl.ds(cc*2*S+128*t,128)],gk,gs,osem.at[1],True,k,2*q+cc,pl.ds(240,128),pl.ds(128*t,128))
    @pl.when(q==1)
    def _():
        pltpu.make_async_copy(dw_s.at[pl.ds(0,960)],dw_s.at[pl.ds(0,960)],osem.at[0]).wait()
        pltpu.make_async_copy(dd_s,dd_s,osem.at[1]).wait()

def ffn_bwd(idx, cb, n2, h, wd, dn2in, gp):
    S=gp[0].shape[3]//2
    full=const((T,DP))
    return pl.pallas_call(functools.partial(ffn_bwd_kernel,S), grid=(2,),
        in_specs=[SMEM,full,full,pl.BlockSpec((1,T,8*S),lambda q:(q,0,0)),pl.BlockSpec((1,4*S,DP),lambda q:(q,0,0)),full]+[ANY]*4,
        out_specs=[full,ANY,ANY],
        out_shape=[sds((T,DP),F32)]+[sds((2,2,4,368,2*S),BF)]*2,
        scratch_shapes=[pltpu.VMEM((8,DP,2*S),BF),pltpu.VMEM((T,8*S),BF),pltpu.VMEM((T,4*S),BF),pltpu.VMEM((DP,8*S),BF),pltpu.VMEM((8,4*S,128),BF),pltpu.SemaphoreType.DMA((2,)),pltpu.SemaphoreType.DMA((2,))],
        compiler_params=params(), cost_estimate=cost(33), name="ffn_bwd")(idx,cb,n2,h,wd,dn2in,*gp)

NEG=-1e30
QB=256
def attn_fwd_kernel(q, k, v, o, lse):
    ri=lax.broadcasted_iota(jnp.int32,(QB,QB),0); ci=lax.broadcasted_iota(jnp.int32,(QB,QB),1)
    for qi in range(T//QB):
        rows=slice(qi*QB,(qi+1)*QB); kn=(qi+1)*QB
        qb=q[0,rows,:]
        s=dot(qb,k[0,0:kn,:],NT)
        sd=jnp.where(ci<=ri,s[:,kn-QB:],NEG)
        s=sd if qi==0 else jnp.concatenate([s[:,:kn-QB],sd],axis=-1)
        m=jnp.max(s,axis=-1,keepdims=True)
        p=jnp.exp(s-m)
        r=dot(p.astype(BF),v[0,0:kn,:])
        l=r[:,64:65]
        o[0,rows,:]=(r/l).astype(BF)
        e=jnp.broadcast_to(m+jnp.log(l),(QB,128))
        lse[0,:,rows]=e.T[0:1,:]

def attn_fwd(q,k,v,g0,ng):
    qs=pl.BlockSpec((1,T,128),lambda g,r:(3*(g+g0)+r,0,0)); ks=pl.BlockSpec((1,T,128),lambda g,r:(g+g0,0,0)); os_=pl.BlockSpec((1,T,128),lambda g,r:(3*g+r,0,0))
    return pl.pallas_call(attn_fwd_kernel,grid=(ng,3),in_specs=[qs,ks,ks],
        out_specs=[os_,pl.BlockSpec((1,1,T),lambda g,r:(3*g+r,0,0))],
        out_shape=[sds((3*ng,T,128),BF),sds((3*ng,1,T),F32)],compiler_params=params(),cost_estimate=cost(6*ng), name="attn_fwd")(q,k,v)

def unrot(g,c,s,low):
    t=jnp.where(low,pltpu.roll(g,96,1),-pltpu.roll(g,32,1))
    return g*c+t*s

def attn_bwd_kernel(q,k,v,do,lse,c,s,dq,dk,dv,dka,dva,dqa):
    r_=pl.program_id(1)
    @pl.when(r_==0)
    def _():
        dka[...]=jnp.zeros_like(dka); dva[...]=jnp.zeros_like(dva)
    ki=lax.broadcasted_iota(jnp.int32,(QB,QB),0); qi_=lax.broadcasted_iota(jnp.int32,(QB,QB),1)
    low=lax.broadcasted_iota(jnp.int32,(QB,128),1)%64<32
    for qi in range(T//QB):
        rows=slice(qi*QB,(qi+1)*QB); kn=(qi+1)*QB
        qb=q[0,rows,:]; dob=do[0,rows,:]; kb=k[0,0:kn,:]
        st=dot(kb,qb,NT)
        pt=jnp.exp(st-lse[0,:,rows])
        pd=jnp.where(ki<=qi_,pt[kn-QB:],0.0)
        pt=pd if qi==0 else jnp.concatenate([pt[:kn-QB],pd],axis=0)
        dpt=dot(v[0,0:kn,:],dob,NT)
        dva[0:kn,:]+=dot(pt.astype(BF),dob)
        t=pt*dpt
        delta=jnp.sum(t,axis=0,keepdims=True)
        dst=(t-pt*delta).astype(BF)
        dka[0:kn,:]+=dot(dst,qb)
        dqr=dot(dst,kb,TN)*0.125
        dq[0,rows,:]=unrot(dqr,c[rows,:],s[rows,:],low).astype(BF)
    @pl.when(r_==2)
    def _():
        for qi in range(T//QB):
            rows=slice(qi*QB,(qi+1)*QB)
            dk[0,rows,:]=unrot(dka[rows,:],c[rows,:],s[rows,:],low).astype(BF)
            dv[0,rows,:]=dva[rows,:].astype(BF)

def attn_bwd(q,k,v,do,lse,c,s,g0,ng):
    qs=pl.BlockSpec((1,T,128),lambda g,r:(3*(g+g0)+r,0,0)); ks=pl.BlockSpec((1,T,128),lambda g,r:(g+g0,0,0))
    qo=pl.BlockSpec((1,T,128),lambda g,r:(3*g+r,0,0)); ko=pl.BlockSpec((1,T,128),lambda g,r:(g,0,0))
    return pl.pallas_call(attn_bwd_kernel,grid=(ng,3),in_specs=[qs,ks,ks,qs,pl.BlockSpec((1,1,T),lambda g,r:(3*g+r,0,0)),const((T,128)),const((T,128))],
        out_specs=[qo,ko,ko],
        out_shape=[sds((3*ng,T,128),BF),sds((ng,T,128),BF),sds((ng,T,128),BF)],
        scratch_shapes=[pltpu.VMEM((T,128),F32),pltpu.VMEM((T,128),F32),pltpu.VMEM((8,128),F32)],
        compiler_params=params(),cost_estimate=cost(9*ng), name="attn_bwd")(q,k,v,do,lse,c,s)

EPS=1e-5
WN=1664
CUT=160
def prefetch(grid,in_specs,out_specs,scratch): return pltpu.PrefetchScalarGridSpec(num_scalar_prefetch=1,grid=grid,in_specs=in_specs,out_specs=out_specs,scratch_shapes=scratch)
def tok(i,idx): return (flip(i%2,idx[3]),flip(i//2,idx[2]),0,0)
tok_spec=lambda: pl.BlockSpec((1,1,D,256),tok)
row_spec=lambda n: pl.BlockSpec((256,n),lambda i,idx:(i,0))
head_spec=lambda h: pl.BlockSpec((h,256,128),lambda i,idx:(0,i,0))
def cst(shape): return pl.BlockSpec(shape,lambda *g:(0,)*len(shape))
def zeros(r,n,dt=F32): return jnp.zeros((r,n),dt)

def qkv_kernel(idx, x, c, s, *refs):
    pa=refs[:4]; pb=refs[4:8]
    n1,q,k,v,w,wo,gains,s1,sem=refs[8:]
    i=pl.program_id(0)
    @pl.when(i==0)
    def _():
        for order,pc,lo,n in (("yx",pa,0,CUT),("xy",pb,CUT,256-CUT)):
            for p,f,xx,ctx,_ in pieces_of(idx,order):
                for dz in range(4):
                    pltpu.make_async_copy(pc[p].at[f,dz], s1.at[lax.rem(idx[0]+dz,4)*2+xx,ctx,pl.ds(lo,n)], sem).start()
        pltpu.make_async_copy(s1,s1,sem).wait()
        for t in range(4):
            rows=slice(240*t,240*t+240)
            w[rows,:]=jnp.concatenate([s1[d,t,0:240,0:120] for d in range(8)]+[s1[d,t,0:240,128:168] for d in range(8)]+[s1[d,t,0:240,168:208] for d in range(8)]+[zeros(240,64,BF)],axis=-1)
            wo[rows,:]=jnp.concatenate([s1[d,t,0:240,256:376] for d in range(8)]+[zeros(240,64,BF)],axis=-1)
        w[960:1024,:]=zeros(64,WN,BF); wo[960:1024,:]=zeros(64,DP,BF)
        gl=[s1[d,t,240:256,0:128].astype(F32)[0:1,0:60] for d in range(8) for t in range(4)]
        gains[0:1,:]=jnp.concatenate(gl[:16]+[zeros(1,64)],axis=-1)
        gains[1:2,:]=jnp.concatenate(gl[16:]+[zeros(1,64)],axis=-1)
    xf=x[:,0:D].astype(F32)
    r=lax.rsqrt(jnp.sum(xf*xf,axis=-1,keepdims=True)*(1.0/D)+EPS)
    n=jnp.concatenate([(xf*r*gains[0:1,0:D]).astype(BF),zeros(256,64,BF)],axis=-1)
    n1[...]=n
    h=dot(n,w[...])
    low=lax.broadcasted_iota(jnp.int32,(256,128),1)%64<32
    z64=zeros(256,64,BF)
    one=jnp.where(lax.broadcasted_iota(jnp.int32,(256,64),1)==0,1.0,0.0).astype(BF)
    for t in range(10):
        g=h[:,128*t:128*t+128]
        u=jnp.where(low,-pltpu.roll(g,96,1),pltpu.roll(g,32,1))
        o=g*c[...]+u*s[...]
        for e in range(2):
            hd=2*t+e
            oh=o[:,64*e:64*e+64]
            if hd<15: q[hd]=jnp.concatenate([(oh*0.125).astype(BF),z64],axis=-1)
            else: k[hd-15]=jnp.concatenate([oh.astype(BF),z64],axis=-1)
    for e in range(5):
        v[e]=jnp.concatenate([h[:,1280+64*e:1344+64*e].astype(BF),one],axis=-1)

def qkv_fwd(idx,x,c,s,pa,pb):
    return pl.pallas_call(qkv_kernel,grid_spec=prefetch((4,),[row_spec(DP),row_spec(128),row_spec(128)]+[ANY]*8,
        [row_spec(DP),head_spec(15),head_spec(5),head_spec(5),cst((DP,WN)),cst((DP,DP)),cst((2,DP))],
        [pltpu.VMEM((8,4,256,384),BF),pltpu.SemaphoreType.DMA]),
        out_shape=[sds((T,DP),BF),sds((15,T,128),BF),sds((5,T,128),BF),sds((5,T,128),BF),sds((DP,WN),BF),sds((DP,DP),BF),sds((2,DP),F32)],
        compiler_params=params(),cost_estimate=cost(16), name="qkv_fwd")(idx,x,c,s,*pa,*pb)

def out_kernel(idx,o1,o2,x,gains,wo,att,mid,n2):
    a=jnp.concatenate([o[h][:,0:64] for o in (o1,o2) for h in range(o.shape[0])]+[zeros(256,64,BF)],axis=-1)
    att[...]=a
    m=dot(a,wo[...])+x[...].astype(F32)
    mid[...]=m
    r=lax.rsqrt(jnp.sum(m*m,axis=-1,keepdims=True)*(1.0/D)+EPS)
    n2[...]=(m*r*gains[1:2,:]).astype(BF)

def out_fwd(idx,o1,o2,x,gains,wo):
    return pl.pallas_call(out_kernel,grid_spec=prefetch((4,),[head_spec(o1.shape[0]),head_spec(o2.shape[0]),row_spec(DP),cst((2,DP)),cst((DP,DP))],
        [row_spec(DP)]*3,[]),out_shape=[sds((T,DP),BF),sds((T,DP),F32),sds((T,DP),BF)],compiler_params=params(),cost_estimate=cost(9), name="out_fwd")(idx,o1,o2,x,gains,wo)

def tok_in_kernel(idx,h,r,g,o):
    y=idx[2]; c=idx[3]
    for ys,cs,v in ((0,0,h[2*y+c]),(1,0,r[c]),(0,1,g[0]),(1,1,g[1])):
        b=2*flip(y,ys)+flip(c,cs)
        o[pl.ds(pl.multiple_of(256*b,256),256),:]=jnp.concatenate([v,zeros(64,256,BF)],axis=0).T
def tok_in(idx,h,r,g):
    return pl.pallas_call(tok_in_kernel,in_specs=[SMEM]+[pl.BlockSpec(memory_space=pltpu.VMEM)]*3,out_specs=pl.BlockSpec(memory_space=pltpu.VMEM),out_shape=sds((T,DP),BF),compiler_params=params(),cost_estimate=cost(4),name="tok_in")(idx,h,r,g)

def out_bwd_kernel(idx,dn2,cb,mid,gains,wo,att,dmid,do,dg,ok,os_,dbr_s,st,sem):
    i=pl.program_id(0)
    m=mid[...]; r=lax.rsqrt(jnp.sum(m*m,axis=-1,keepdims=True)*(1.0/D)+EPS)
    d=dn2[...]; gd=gains[1:2,:]*d
    dm=cb[...].astype(F32)+r*gd-m*(r*r*r)*(jnp.sum(gd*m,axis=-1,keepdims=True)*(1.0/D))
    dmid[...]=dm
    g=jnp.sum(d*m*r,axis=0,keepdims=True)
    dg[...]=g+jnp.where(i==0,0.0,dg[...])
    b=dm.astype(BF)
    dbr_s[pl.ds(pl.multiple_of(i*256,256),256),:]=b
    da=dot(b,wo[...],NT)
    z64=zeros(256,64,BF)
    for h in range(15): do[h]=jnp.concatenate([da[:,64*h:64*h+64].astype(BF),z64],axis=-1)
    @pl.when(i==3)
    def _():
        for mm in range(4):
            rr=dot(att[:,256*mm:256*mm+256],dbr_s[...],TN)
            for k in range(8):
                st[k,256*mm:256*mm+256,:]=jnp.concatenate([rr[:,120*k:120*k+120],zeros(256,8)],axis=-1).astype(BF)
        for k in range(8):
            for t in range(4):
                put(idx,st.at[k,pl.ds(240*t,CUT)],ok,os_,sem,False,k,t,pl.ds(0,CUT)); put(idx,st.at[k,pl.ds(240*t+CUT,240-CUT)],ok,os_,sem,True,k,t,pl.ds(CUT,240-CUT))
        pltpu.make_async_copy(st.at[:,pl.ds(0,960)],st.at[:,pl.ds(0,960)],sem).wait()

def out_bwd(idx,dn2,cb,mid,gains,wo,att):
    return pl.pallas_call(out_bwd_kernel,grid_spec=prefetch((4,),[row_spec(DP)]*3+[cst((2,DP)),cst((DP,DP)),cst((T,DP))],
        [row_spec(DP),head_spec(15),cst((1,DP)),ANY,ANY],[pltpu.VMEM((T,DP),BF),pltpu.VMEM((8,DP,128),BF),pltpu.SemaphoreType.DMA]),
        out_shape=[sds((T,DP),F32),sds((15,T,128),BF),sds((1,DP),F32)]+[sds((2,2,4,240,128),BF)]*2,
        compiler_params=params(),cost_estimate=cost(16), name="out_bwd")(idx,dn2,cb,mid,gains,wo,att)

def qkv_bwd_kernel(idx,dq1,dk1,dv1,dq2,dk2,dv2,x,gains,n1,dmid,w,dg2,hg,wk,ws,dh_s,st,sg,dg1,sem):
    i=pl.program_id(0)
    dh=jnp.concatenate([r[h][:,0:64] for r in (dq1,dq2,dk1,dk2,dv1,dv2) for h in range(r.shape[0])]+[zeros(256,64,BF)],axis=-1)
    dh_s[pl.ds(pl.multiple_of(i*256,256),256),:]=dh
    d=dot(dh,w[...],NT)[:,0:D]
    xf=x[:,0:D].astype(F32)
    r=lax.rsqrt(jnp.sum(xf*xf,axis=-1,keepdims=True)*(1.0/D)+EPS)
    gd=gains[0:1,0:D]*d
    hh=dmid[:,0:D]+r*gd-xf*(r*r*r)*(jnp.sum(gd*xf,axis=-1,keepdims=True)*(1.0/D))
    hg[0,0]=jnp.concatenate([hh,zeros(256,64)],axis=-1).T[:D,:].astype(BF)
    g=jnp.sum(d*xf*r,axis=0,keepdims=True)
    dg1[...]=g+jnp.where(i==0,0.0,dg1[...])
    @pl.when(i==3)
    def _():
        for m in range(4):
            r_=dot(n1[:,256*m:256*m+256],dh_s[...],TN)
            for k in range(8):
                st[k,256*m:256*m+256,:]=jnp.concatenate([r_[:,120*k:120*k+120],zeros(256,8),r_[:,960+40*k:1000+40*k],r_[:,1280+40*k:1320+40*k],zeros(256,48)],axis=-1).astype(BF)
        sg[...]=jnp.zeros_like(sg)
        for k in range(8):
            for t in range(4):
                o=(4*k+t)*60
                src=dg1[:,o:o+60] if k<4 else dg2[:,o-960:o-900]
                sg[k,t,:,0:128]=jnp.broadcast_to(jnp.concatenate([src,zeros(1,68)],axis=-1),(16,128)).astype(BF)
                c,xx,y,z=slot_of(idx,k,t)
                def go(dst):
                    pltpu.make_async_copy(st.at[k,pl.ds(240*t,CUT)],dst.at[xx,y,z,pl.ds(0,CUT)],sem).start()
                    pltpu.make_async_copy(st.at[k,pl.ds(240*t+CUT,240-CUT)],dst.at[y,xx,z,pl.ds(CUT,240-CUT)],sem).start()
                    pltpu.make_async_copy(sg.at[k,t],dst.at[y,xx,z,pl.ds(240,16)],sem).start()
                @pl.when(c==0)
                def _(): go(wk)
                @pl.when(c==1)
                def _(): go(ws)
        pltpu.make_async_copy(st.at[:,pl.ds(0,960)],st.at[:,pl.ds(0,960)],sem).wait()
        pltpu.make_async_copy(sg,sg,sem).wait()

def qkv_bwd(idx,g1,g2,x,gains,n1,dmid,w,dg2):
    return pl.pallas_call(qkv_bwd_kernel,grid_spec=prefetch((4,),[head_spec(a.shape[0]) for a in (*g1,*g2)]+[row_spec(DP),cst((2,DP)),cst((T,DP)),row_spec(DP),cst((DP,WN)),cst((1,DP))],
        [tok_spec(),ANY,ANY],[pltpu.VMEM((T,WN),BF),pltpu.VMEM((8,DP,256),BF),pltpu.VMEM((8,4,16,256),BF),pltpu.VMEM((1,D),F32),pltpu.SemaphoreType.DMA]),
        out_shape=[sds((2,2,D,256),BF)]+[sds((2,2,4,256,256),BF)]*2,
        compiler_params=params(),cost_estimate=cost(18), name="qkv_bwd")(idx,*g1,*g2,x,gains,n1,dmid,w,dg2)

def tok_out_kernel(idx,a,r,b,o):
    y=idx[2]; c=idx[3]
    o[2*y+c]=a[0,0]; o[2*y+1-c]=r[0]
    o[2*(1-y)+c]=b[0]; o[2*(1-y)+1-c]=b[1]
def tok_out(idx,a,r,b):
    v=pl.BlockSpec(memory_space=pltpu.VMEM)
    return pl.pallas_call(tok_out_kernel,grid=(1,),in_specs=[SMEM,pl.BlockSpec((1,1,D,256),lambda i:(0,0,0,0)),pl.BlockSpec((1,D,256),lambda i:(0,0,0)),v],out_specs=v,out_shape=sds((4,D,256),BF),compiler_params=params(),cost_estimate=cost(4),name="tok_out")(idx,a,r,b)


def swap(a, axis, bit):
    n = lax.axis_size(axis)
    return lax.ppermute(a, axis, [(i, i ^ bit) for i in range(n)])

def move(a, name):
    if name == "x": return swap(a, "dp", 1)
    if name == "y": return swap(a, "ctx", 2)
    return swap(a, "ctx", 1)

def from_z(a, k):
    return lax.ppermute(a, "dp", [(((z + k) % 4) * 2 + x, z * 2 + x) for z in range(4) for x in range(2)])

def after(a, *others):
    return lax.optimization_barrier((a,) + others)[0]

def gather_z(shard, cut):
    ps = [shard] + [from_z(shard, k) for k in (1, 2, 3)]
    return jnp.stack([p[:cut] for p in ps]), jnp.stack([p[cut:] for p in ps])

def gather_first(g):
    a, b = g
    return jnp.stack([a, move(a, "y")]), jnp.stack([b, move(b, "x")])

def gather_second(g):
    a, b = g
    return (a, move(a, "x")), (b, move(b, "y"))

def gather_core(g):
    return [list(h) + [move(p, "c") for p in h] for h in g]

def add(*terms):
    total = terms[0].astype(F32)
    for t in terms[1:]: total = total + t.astype(F32)
    return total

def reduce_core(send):
    return move(send, "c")

def reduce_first(keep, rc, cut):
    low = add(keep[1], rc[1]).astype(BF)
    return move(low[:, :, :cut], "x"), move(low[:, :, cut:], "y")

def reduce_second(keep, rc, r1, cut):
    a, b = r1
    low = add(keep[0, 1], rc[0, 1])
    return (move((low[:, :cut] + a[1].astype(F32)).astype(BF), "y"),
            move((low[:, cut:] + b[1].astype(F32)).astype(BF), "x"))

def reduce_z(keep, rc, r1, r2):
    own = add(keep[0, 0], rc[0, 0], jnp.concatenate([r1[0][0], r1[1][0]], axis=1), jnp.concatenate(r2, axis=1))
    low = own.astype(BF)
    return own[0], [from_z(low[k], 4 - k) for k in (1, 2, 3)]

def exchange_in_y(idx, a):
    return move(lax.dynamic_slice_in_dim(a, 2 * (1 - idx[2]), 2, 0), "y")

def exchange_in_c(idx, a, r):
    y, c = idx[2], idx[3]
    give = jnp.concatenate([lax.dynamic_slice_in_dim(a, 2 * y + 1 - c, 1, 0), lax.dynamic_slice_in_dim(r, 1 - c, 1, 0)])
    return move(give, "c")

SPLIT = ((0, 192), (192, 320))

def fast(hidden_in, norm_gains, w_query, w_key, w_value, w_out, w_gate, w_up, w_down, cotangent):
    di, ci = lax.axis_index("dp"), lax.axis_index("ctx")
    idx = jnp.stack([di // 2, di % 2, ci // 2, ci % 2]).astype(jnp.int32)
    pz = lambda r, n: jnp.zeros((r, n), BF)
    c1 = jnp.concatenate([w_query, pz(240, 8), w_key, w_value, pz(240, 48), w_out, pz(240, 8)], axis=1)
    gain_row = jnp.pad(norm_gains.reshape(1, 60), ((0, 15), (0, 324)))
    c1 = jnp.concatenate([c1, gain_row], axis=0)
    def pack(lo, hi):
        s = hi - lo
        gu = jnp.concatenate([w_gate[:, lo:hi], w_up[:, lo:hi]], axis=1)
        d = jnp.concatenate([w_down[lo:hi], w_down[320 + lo:320 + hi]], axis=0)
        d = jnp.pad(d, ((0, 0), (0, 8)))
        d = jnp.concatenate([d[128 * t:128 * t + 128] for t in range(2 * s // 128)], axis=1)
        return jnp.concatenate([gu, d], axis=0)
    ht, ct = jnp.swapaxes(hidden_in, 1, 2), jnp.swapaxes(cotangent, 1, 2)
    xr = exchange_in_y(idx, ht)
    g1 = gather_z(c1, CUT)
    ga = gather_z(after(pack(*SPLIT[0]), g1[0]), 240)
    gb = gather_z(after(pack(*SPLIT[1]), ga[0]), 240)
    xg = exchange_in_c(idx, ht, xr)
    x = tok_in(idx, ht, xr, xg)
    p1 = gather_core(gather_second(gather_first(g1)))
    pa = gather_core(gather_second(gather_first(ga)))
    pb = gather_core(gather_second(gather_first(gb)))
    cr = exchange_in_y(idx, ct)
    cg = exchange_in_c(idx, ct, cr)
    cos, sin = rope_tables(jnp.arange(T).astype(F32), HD)
    cos, sin = jnp.tile(cos, (1, 2)), jnp.tile(sin, (1, 2))
    n1, q, k, v, w, wo, gains = qkv_fwd(idx, x, cos, sin, *p1)
    o1, lse1 = attn_fwd(q, k, v, 0, 3)
    o2, lse2 = attn_fwd(q, k, v, 3, 2)
    att, mid, n2 = out_fwd(idx, o1, o2, x, gains, wo)
    acc, ha, wda = ffn_fwd(idx, n2, mid, *pa, False)
    out, hb, wdb = ffn_fwd(idx, n2, acc, *pb, True)
    cb = tok_in(idx, ct, cr, cg)
    hr = move(out[1], "c")
    hb_ = move(jnp.stack([out[0, 1], hr[1]]), "y")
    hidden_out = tok_out(idx, out, hr, hb_)
    dn2, ka, sa = ffn_bwd(idx, cb, n2, ha, wda, jnp.zeros((T, DP), F32), pa[0])
    ra_c = reduce_core(sa)
    dn2, kb, sb = ffn_bwd(idx, cb, n2, hb, wdb, dn2, pb[0])
    rb_c = reduce_core(sb)
    dmid, do, dg2, ko, so = out_bwd(idx, dn2, cb, mid, gains, wo, att)
    ro_c = reduce_core(so)
    b1 = attn_bwd(q, k, v, do, lse1, cos, sin, 0, 3)
    b2 = attn_bwd(q, k, v, do, lse2, cos, sin, 3, 2)
    hg, kq, sq = qkv_bwd(idx, b1, b2, x, gains, n1, dmid, w, dg2)
    rq_c = reduce_core(sq)
    gr = move(hg[1], "c")
    gb_ = move(jnp.stack([hg[0, 1], gr[1]]), "y")
    hidden_grad = tok_out(idx, hg, gr, gb_)
    factor = 1.0 / math.sqrt(lax.axis_size("dp") * hidden_in.shape[0] * T)
    def finish(keep, rc, cut):
        r1 = reduce_first(keep, rc, cut)
        r2 = reduce_second(keep, rc, r1, cut)
        own, others = reduce_z(keep, rc, r1, r2)
        return add(own, *others) * factor
    ra = finish(ka, ra_c, 240)
    rb = finish(kb, rb_c, 240)
    ro = finish(ko, ro_c, CUT)
    rq = finish(kq, rq_c, CUT)
    gate, up, down = [], [], []
    for (lo, hi), r in zip(SPLIT, (ra, rb)):
        s = hi - lo
        gate.append(r[:240, :s]); up.append(r[:240, s:])
        d = jnp.concatenate([r[240:, 128 * t:128 * t + 128] for t in range(2 * s // 128)], axis=0)[:, :120]
        down.append((d[:s], d[s:]))
    return (jnp.swapaxes(hidden_out, 1, 2), jnp.swapaxes(hidden_grad, 1, 2), rq[240, :60], rq[:240, :120], rq[:240, 128:168],
            rq[:240, 168:208], ro[:, :120], jnp.concatenate(gate, axis=1), jnp.concatenate(up, axis=1),
            jnp.concatenate([down[0][0], down[1][0], down[0][1], down[1][1]], axis=0))


def body(hidden_in, *rest):
    seqs_here, seg_len, _ = hidden_in.shape
    if (lax.axis_size("dp"), lax.axis_size("ctx"), seqs_here, seg_len) == (8, 4, 4, 256):
        return fast(hidden_in, *rest)
    return local(hidden_in, *rest)


def solution(mesh):
    in_specs = (
        P("dp", "ctx", None),
        P(("dp", "ctx")),
        P("ctx", "dp"),
        P("ctx", "dp"),
        P("ctx", "dp"),
        P("ctx", "dp"),
        P("ctx", "dp"),
        P("ctx", "dp"),
        P("ctx", "dp"),
        P("dp", "ctx", None),
    )
    out_specs = (
        P("dp", "ctx", None),
        P("dp", "ctx", None),
        P(("dp", "ctx")),
        P("ctx", "dp"),
        P("ctx", "dp"),
        P("ctx", "dp"),
        P("ctx", "dp"),
        P("ctx", "dp"),
        P("ctx", "dp"),
        P("ctx", "dp"),
    )
    return jax.shard_map(body, mesh=mesh, in_specs=in_specs, out_specs=out_specs, check_vma=False)
```

```python
import functools
import math

import jax
import jax.numpy as jnp
from jax import lax
from jax.experimental import pallas as pl
from jax.experimental.pallas import tpu as pltpu
from jax.sharding import PartitionSpec as P


QH = 15
KVH = 5
HD = 64


epsilon = 1e-05
rope_base = 100000.0
masked_score = -1e30
contract_last = (((1,), (1,)), ((), ()))
contract_first = (((0,), (0,)), ((), ()))


def rope_tables(positions, head_size):
    half_size = head_size // 2
    frequencies = jnp.exp(
        -(jnp.arange(half_size).astype(jnp.float32) * (2.0 / head_size)) * math.log(rope_base)
    )
    angles = positions[:, None] * frequencies[None, :]
    angles = jnp.concatenate([angles, angles], axis=-1)
    return (jnp.cos(angles), jnp.sin(angles))


def rotate(values, cos_table, sin_table):
    half_size = values.shape[-1] // 2
    turned = jnp.concatenate([-values[..., half_size:], values[..., :half_size]], axis=-1)
    return values * cos_table[:, None, :] + turned * sin_table[:, None, :]


def unrotate(grad_turned, cos_table, sin_table):
    _, pullback = jax.vjp(lambda values: rotate(values, cos_table, sin_table), grad_turned)
    return pullback(grad_turned)[0]


def rms_scale(values, gain_row):
    return (
        values * lax.rsqrt(jnp.mean(values * values, axis=-1, keepdims=True) + epsilon) * gain_row
    )


def local(hidden_in, norm_gains, w_query, w_key, w_value, w_out, w_gate, w_up, w_down, cotangent):
    seqs_here, seg_len, model_width = hidden_in.shape
    ctx_size = lax.axis_size("ctx")
    dp_size = lax.axis_size("dp")
    full_len = seg_len * ctx_size
    rows_here = seqs_here * seg_len
    per_group = QH // KVH
    score_scale = HD ** (-0.5)
    row_parts = (
        lax.all_gather(w_query, "ctx", axis=0, tiled=True),
        lax.all_gather(w_key, "ctx", axis=0, tiled=True),
        lax.all_gather(w_value, "ctx", axis=0, tiled=True),
        lax.all_gather(w_out, "ctx", axis=0, tiled=True),
        lax.all_gather(w_gate, "ctx", axis=0, tiled=True),
        lax.all_gather(w_up, "ctx", axis=0, tiled=True),
        lax.all_gather(w_down, "ctx", axis=0, tiled=True),
        lax.all_gather(norm_gains.reshape(-1, 1), "ctx", axis=0, tiled=True),
    )
    gathered = (
        lax.all_gather(row_parts[0], "dp", axis=1, tiled=True),
        lax.all_gather(row_parts[1], "dp", axis=1, tiled=True),
        lax.all_gather(row_parts[2], "dp", axis=1, tiled=True),
        lax.all_gather(row_parts[3], "dp", axis=1, tiled=True),
        lax.all_gather(row_parts[4], "dp", axis=1, tiled=True),
        lax.all_gather(row_parts[5], "dp", axis=1, tiled=True),
        lax.all_gather(row_parts[6], "dp", axis=1, tiled=True),
        lax.all_gather(row_parts[7].reshape(1, -1), "dp", axis=1, tiled=True),
    )
    first_pos = lax.axis_index("ctx") * seg_len + jnp.arange(seg_len)
    cos_table, sin_table = rope_tables(first_pos.astype(jnp.float32), HD)
    row_pos = jnp.tile(first_pos, per_group)
    causal_mask = jnp.arange(full_len)[None, :] <= row_pos[:, None]

    def group_queries(tensor):
        return (
            tensor.reshape(seqs_here, seg_len, KVH, per_group, HD)
            .transpose(0, 2, 3, 1, 4)
            .reshape(seqs_here * KVH, per_group * seg_len, HD)
        )

    def ungroup_queries(tensor):
        return (
            tensor.reshape(seqs_here, KVH, per_group, seg_len, HD)
            .transpose(0, 3, 1, 2, 4)
            .reshape(rows_here, QH * HD)
        )

    def group_keys(tensor):
        return (
            tensor.reshape(seqs_here, full_len, KVH, HD)
            .transpose(0, 2, 1, 3)
            .reshape(seqs_here * KVH, full_len, HD)
        )

    def ungroup_keys(tensor):
        return (
            tensor.reshape(seqs_here, KVH, full_len, HD)
            .transpose(0, 2, 1, 3)
            .reshape(seqs_here, full_len, KVH * HD)
        )

    def block_scores(query_block, key_block):
        raw_scores = (
            lax.dot_general(
                query_block, key_block, contract_last, preferred_element_type=jnp.float32
            )
            * score_scale
        )
        return jnp.where(causal_mask, raw_scores, masked_score)

    def attend_forward(triple):
        query_block, key_block, value_block = triple
        scores = block_scores(query_block, key_block)
        row_top = jnp.max(scores, axis=-1, keepdims=True)
        exponents = jnp.exp(scores - row_top)
        totals = jnp.sum(exponents, axis=-1, keepdims=True)
        attn_weights = exponents / totals
        attended = jnp.dot(
            attn_weights.astype(jnp.bfloat16), value_block, preferred_element_type=jnp.float32
        )
        return (attended, (row_top + jnp.log(totals))[:, 0])

    gains_full = gathered[7].reshape(-1).astype(jnp.float32)
    inputs_f32 = hidden_in.reshape(rows_here, model_width).astype(jnp.float32)
    normed = rms_scale(inputs_f32, gains_full[:model_width]).astype(jnp.bfloat16)
    queries = jnp.dot(normed, gathered[0], preferred_element_type=jnp.float32).reshape(
        seqs_here, seg_len, QH, HD
    )
    key_proj = jnp.dot(normed, gathered[1], preferred_element_type=jnp.float32).reshape(
        seqs_here, seg_len, KVH, HD
    )
    value_proj = (
        jnp.dot(normed, gathered[2], preferred_element_type=jnp.float32)
        .astype(jnp.bfloat16)
        .reshape(seqs_here, seg_len, KVH * HD)
    )
    turned_query = rotate(queries, cos_table, sin_table).astype(jnp.bfloat16)
    turned_key = (
        rotate(key_proj, cos_table, sin_table)
        .astype(jnp.bfloat16)
        .reshape(seqs_here, seg_len, KVH * HD)
    )
    key_sets = (
        lax.all_gather(turned_key, "ctx", axis=1, tiled=True),
        lax.all_gather(value_proj, "ctx", axis=1, tiled=True),
    )
    grouped_query = group_queries(turned_query)
    attended, log_totals = lax.map(
        attend_forward, (grouped_query, group_keys(key_sets[0]), group_keys(key_sets[1]))
    )
    mixed_heads = ungroup_queries(attended).astype(jnp.bfloat16)
    middle = inputs_f32 + jnp.dot(mixed_heads, gathered[3], preferred_element_type=jnp.float32)
    normed_two = rms_scale(middle, gains_full[model_width:]).astype(jnp.bfloat16)
    gate_pre = jnp.dot(normed_two, gathered[4], preferred_element_type=jnp.float32)
    up_pre = jnp.dot(normed_two, gathered[5], preferred_element_type=jnp.float32)
    product = (jax.nn.silu(gate_pre) * up_pre).astype(jnp.bfloat16)
    result = middle + jnp.dot(product, gathered[6], preferred_element_type=jnp.float32)
    hidden_out = result.astype(jnp.bfloat16).reshape(seqs_here, seg_len, model_width)
    rows_again = (
        lax.all_gather(w_query, "ctx", axis=0, tiled=True),
        lax.all_gather(w_key, "ctx", axis=0, tiled=True),
        lax.all_gather(w_value, "ctx", axis=0, tiled=True),
        lax.all_gather(w_out, "ctx", axis=0, tiled=True),
        lax.all_gather(w_gate, "ctx", axis=0, tiled=True),
        lax.all_gather(w_up, "ctx", axis=0, tiled=True),
        lax.all_gather(w_down, "ctx", axis=0, tiled=True),
        lax.all_gather(norm_gains.reshape(-1, 1), "ctx", axis=0, tiled=True),
    )
    refetched = (
        lax.all_gather(rows_again[0], "dp", axis=1, tiled=True),
        lax.all_gather(rows_again[1], "dp", axis=1, tiled=True),
        lax.all_gather(rows_again[2], "dp", axis=1, tiled=True),
        lax.all_gather(rows_again[3], "dp", axis=1, tiled=True),
        lax.all_gather(rows_again[4], "dp", axis=1, tiled=True),
        lax.all_gather(rows_again[5], "dp", axis=1, tiled=True),
        lax.all_gather(rows_again[6], "dp", axis=1, tiled=True),
        lax.all_gather(rows_again[7].reshape(1, -1), "dp", axis=1, tiled=True),
    )
    keys_again = (
        lax.all_gather(turned_key, "ctx", axis=1, tiled=True),
        lax.all_gather(value_proj, "ctx", axis=1, tiled=True),
    )
    gains_back = refetched[7].reshape(-1).astype(jnp.float32)
    seed_low = cotangent.reshape(rows_here, model_width)
    seed_high = seed_low.astype(jnp.float32)
    down_part = lax.dot_general(
        product, seed_low, contract_first, preferred_element_type=jnp.float32
    )
    grad_product = lax.dot_general(
        seed_low, refetched[6], contract_last, preferred_element_type=jnp.float32
    )
    _, gate_pull = jax.vjp(
        lambda gate_in, up_in: jax.nn.silu(gate_in) * up_in, gate_pre, up_pre
    )
    grad_gate, grad_up = gate_pull(grad_product)
    grad_gate = grad_gate.astype(jnp.bfloat16)
    grad_up = grad_up.astype(jnp.bfloat16)
    gate_part = lax.dot_general(
        normed_two, grad_gate, contract_first, preferred_element_type=jnp.float32
    )
    up_part = lax.dot_general(
        normed_two, grad_up, contract_first, preferred_element_type=jnp.float32
    )
    grad_normed_two = lax.dot_general(
        grad_gate, refetched[4], contract_last, preferred_element_type=jnp.float32
    ) + lax.dot_general(grad_up, refetched[5], contract_last, preferred_element_type=jnp.float32)
    _, second_pull = jax.vjp(rms_scale, middle, gains_back[model_width:])
    grad_middle_norm, gain_two_part = second_pull(grad_normed_two)
    grad_middle = seed_high + grad_middle_norm
    grad_branch = grad_middle.astype(jnp.bfloat16)
    out_part = lax.dot_general(
        mixed_heads, grad_branch, contract_first, preferred_element_type=jnp.float32
    )
    grad_mixed = lax.dot_general(
        grad_branch, refetched[3], contract_last, preferred_element_type=jnp.float32
    ).astype(jnp.bfloat16)

    def attend_backward(bundle):
        query_block, key_block, value_block, log_total, grad_block = bundle
        scores = block_scores(query_block, key_block)
        attn_weights = jnp.exp(scores - log_total[:, None])
        grad_weights = lax.dot_general(
            grad_block, value_block, contract_last, preferred_element_type=jnp.float32
        )
        grad_values = lax.dot_general(
            attn_weights.astype(jnp.bfloat16),
            grad_block,
            contract_first,
            preferred_element_type=jnp.float32,
        )
        grad_scores = (
            attn_weights
            * (grad_weights - jnp.sum(attn_weights * grad_weights, axis=-1, keepdims=True))
        ).astype(jnp.bfloat16)
        grad_queries = (
            jnp.dot(grad_scores, key_block, preferred_element_type=jnp.float32) * score_scale
        )
        grad_keys = (
            lax.dot_general(
                grad_scores, query_block, contract_first, preferred_element_type=jnp.float32
            )
            * score_scale
        )
        return (grad_queries, grad_keys, grad_values)

    grad_grouped = group_queries(grad_mixed.reshape(seqs_here, seg_len, QH, HD))
    query_blocks, key_blocks, value_blocks = lax.map(
        attend_backward,
        (
            grouped_query,
            group_keys(keys_again[0]),
            group_keys(keys_again[1]),
            log_totals,
            grad_grouped,
        ),
    )
    key_sums = (
        lax.psum_scatter(ungroup_keys(key_blocks), "ctx", scatter_dimension=1, tiled=True),
        lax.psum_scatter(ungroup_keys(value_blocks), "ctx", scatter_dimension=1, tiled=True),
    )
    grad_query = (
        unrotate(
            ungroup_queries(query_blocks).reshape(seqs_here, seg_len, QH, HD), cos_table, sin_table
        )
        .astype(jnp.bfloat16)
        .reshape(rows_here, QH * HD)
    )
    grad_key = (
        unrotate(key_sums[0].reshape(seqs_here, seg_len, KVH, HD), cos_table, sin_table)
        .astype(jnp.bfloat16)
        .reshape(rows_here, KVH * HD)
    )
    grad_value = key_sums[1].astype(jnp.bfloat16).reshape(rows_here, KVH * HD)
    query_part = lax.dot_general(
        normed, grad_query, contract_first, preferred_element_type=jnp.float32
    )
    key_part = lax.dot_general(normed, grad_key, contract_first, preferred_element_type=jnp.float32)
    value_part = lax.dot_general(
        normed, grad_value, contract_first, preferred_element_type=jnp.float32
    )
    grad_normed = (
        lax.dot_general(grad_query, refetched[0], contract_last, preferred_element_type=jnp.float32)
        + lax.dot_general(grad_key, refetched[1], contract_last, preferred_element_type=jnp.float32)
        + lax.dot_general(
            grad_value, refetched[2], contract_last, preferred_element_type=jnp.float32
        )
    )
    _, first_pull = jax.vjp(rms_scale, inputs_f32, gains_back[:model_width])
    grad_inputs_norm, gain_one_part = first_pull(grad_normed)
    hidden_grad = (
        (grad_middle + grad_inputs_norm)
        .astype(jnp.bfloat16)
        .reshape(seqs_here, seg_len, model_width)
    )
    gain_part = jnp.concatenate([gain_one_part, gain_two_part])
    col_sums = (
        lax.psum_scatter(query_part, "dp", scatter_dimension=1, tiled=True),
        lax.psum_scatter(key_part, "dp", scatter_dimension=1, tiled=True),
        lax.psum_scatter(value_part, "dp", scatter_dimension=1, tiled=True),
        lax.psum_scatter(out_part, "dp", scatter_dimension=1, tiled=True),
        lax.psum_scatter(gate_part, "dp", scatter_dimension=1, tiled=True),
        lax.psum_scatter(up_part, "dp", scatter_dimension=1, tiled=True),
        lax.psum_scatter(down_part, "dp", scatter_dimension=1, tiled=True),
        lax.psum_scatter(gain_part.reshape(1, -1), "dp", scatter_dimension=1, tiled=True),
    )
    owned = (
        lax.psum_scatter(col_sums[0], "ctx", scatter_dimension=0, tiled=True),
        lax.psum_scatter(col_sums[1], "ctx", scatter_dimension=0, tiled=True),
        lax.psum_scatter(col_sums[2], "ctx", scatter_dimension=0, tiled=True),
        lax.psum_scatter(col_sums[3], "ctx", scatter_dimension=0, tiled=True),
        lax.psum_scatter(col_sums[4], "ctx", scatter_dimension=0, tiled=True),
        lax.psum_scatter(col_sums[5], "ctx", scatter_dimension=0, tiled=True),
        lax.psum_scatter(col_sums[6], "ctx", scatter_dimension=0, tiled=True),
        lax.psum_scatter(col_sums[7].reshape(-1, 1), "ctx", scatter_dimension=0, tiled=True),
    )
    factor = 1.0 / math.sqrt(dp_size * seqs_here * full_len)
    return (
        hidden_out,
        hidden_grad,
        owned[7].reshape(-1) * factor,
        owned[0] * factor,
        owned[1] * factor,
        owned[2] * factor,
        owned[3] * factor,
        owned[4] * factor,
        owned[5] * factor,
        owned[6] * factor,
    )


BF=jnp.bfloat16; F32=jnp.float32
T=1024; D=960; DP=1024
NT=(((1,),(1,)),((),())); NN=(((1,),(0,)),((),())); TN=(((0,),(0,)),((),()))
def dot(a,b,dn=NN): return lax.dot_general(a,b,dn,preferred_element_type=F32)
ANY=pl.BlockSpec(memory_space=pl.ANY)
SMEM=pl.BlockSpec(memory_space=pltpu.SMEM)
def flip(a,b): return lax.bitwise_xor(a,b)
def const(shape): return pl.BlockSpec(shape,lambda *g:(0,)*len(shape))
def params(): return pltpu.CompilerParams(vmem_limit_bytes=60<<20)
def cost(us): return pl.CostEstimate(flops=int(us*9e8),bytes_accessed=int(us*2e6),transcendentals=0)
def sds(shape,dt): return jax.ShapeDtypeStruct(shape,dt)

def places(idx, kind, pieces):
    for dc in range(2):
        for dx in range(2):
            for dy in range(2):
                for dz in range(4):
                    src=pieces[4*dc+2*dx+dy].at[dz] if kind=="z" else pieces[4*dc+dz].at[2*dx+dy]
                    z=lax.rem(idx[0]+dz,4); y=flip(idx[2],dy)
                    yield src, 2*z+flip(idx[1],dx), 2*y+flip(idx[3],dc), z, y

def load_rows(idx, kind, pieces, dst, sem):
    for src,dpi,ctx,z,_ in places(idx,kind,pieces):
        pltpu.make_async_copy(src.at[pl.ds(0,240)], dst.at[dpi,pl.ds(pl.multiple_of(ctx*240,16),240)], sem.at[z//2]).start()

def wait_rows(dst, sem, j):
    half=dst.at[pl.ds(4*j,4),pl.ds(0,960)]
    pltpu.make_async_copy(half,half,sem.at[j]).wait()

def load_cols(idx, kind, pieces, dst, sem):
    for src,dpi,ctx,_,y in places(idx,kind,pieces):
        for t in range(dst.shape[2]//128):
            pltpu.make_async_copy(src.at[pl.ds(240,128),pl.ds(128*t,128)], dst.at[ctx,dpi,pl.ds(128*t,128)], sem.at[y]).start()

def wait_cols(dst, sem, j):
    half=dst.at[pl.ds(2*j,2)]
    pltpu.make_async_copy(half,half,sem.at[j]).wait()

def ffn_fwd_kernel(S, kind, last, idx, n2, mid, *refs):
    gp=refs[:8]
    out, h_ref, wd_ref, gu_s, d_s, acc, sem = refs[8:]
    j=pl.program_id(0); i=pl.program_id(1)
    @pl.when((j==0)&(i==0))
    def _():
        load_rows(idx,kind,gp,gu_s,sem.at[0])
        load_cols(idx,kind,gp,d_s,sem.at[1])
    @pl.when(i==0)
    def _():
        wait_rows(gu_s,sem.at[0],j); wait_cols(d_s,sem.at[1],j)
        for k in range(4): gu_s[4*j+k,960:1024,:]=jnp.zeros((64,2*S),BF)
        for b in range(2):
            wd_ref[0,b*2*S:(b+1)*2*S,:]=jnp.concatenate([d_s[2*j+b,k][:,:120] for k in range(8)]+[jnp.zeros((2*S,64),BF)],axis=-1)
    rows=pl.ds(pl.multiple_of(i*256,256),256)
    xb=n2[rows,:]
    acts=[]
    for q in range(2):
        w=jnp.concatenate([gu_s[4*j+2*q],gu_s[4*j+2*q+1]],axis=-1)
        h=dot(xb,w)
        h_ref[0,:,q*4*S:(q+1)*4*S]=h.astype(BF)
        for b in range(2):
            g=h[:,b*2*S:b*2*S+S]; u=h[:,b*2*S+S:b*2*S+2*S]
            acts.append((g/(1+jnp.exp(-g))*u).astype(BF))
    act=jnp.concatenate(acts,axis=-1)
    o=dot(act,wd_ref[0])
    @pl.when(j==0)
    def _(): acc[rows,:]=o+mid[rows,:]
    @pl.when(j==1)
    def _():
        r=acc[rows,:]+o
        if last: out[0,0]=r.T[:D,:].astype(BF)
        else: out[...]=r

def ffn_fwd(idx, n2, mid, gp, kind, last):
    S=gp[0].shape[2]//2
    full=pl.BlockSpec((T,DP),lambda j,i,idx:(0,0))
    if last: ospec=pl.BlockSpec((1,1,D,256),lambda j,i,idx:(flip((i*j)%2,idx[3]),flip((i*j)//2,idx[2]),0,0))
    else: ospec=pl.BlockSpec((256,DP),lambda j,i,idx:(i*j,0))
    return pl.pallas_call(functools.partial(ffn_fwd_kernel,S,kind,last), grid_spec=pltpu.PrefetchScalarGridSpec(num_scalar_prefetch=1,grid=(2,4),
        in_specs=[full,full]+[ANY]*8,
        out_specs=[ospec, pl.BlockSpec((1,256,8*S),lambda j,i,idx:(j,i,0)), pl.BlockSpec((1,4*S,DP),lambda j,i,idx:(j,0,0))],
        scratch_shapes=[pltpu.VMEM((8,DP,2*S),BF),pltpu.VMEM((4,8,2*S,128),BF),pltpu.VMEM((T,DP),F32),pltpu.SemaphoreType.DMA((2,2))]),
        out_shape=[sds((2,2,D,256),BF) if last else sds((T,DP),F32),sds((2,T,8*S),BF),sds((2,4*S,DP),BF)],
        compiler_params=params(), cost_estimate=cost(20), name="ffn_fwd")(idx,n2,mid,*gp)

def slot_of(idx, dpi, ctx):
    z=dpi//2; x=dpi%2; y=ctx//2; c=ctx%2
    return flip(c,idx[3]), flip(x,idx[1]), flip(y,idx[2]), lax.rem(z-idx[0]+4,4)

def put(idx, src, keep, send, sem, dpi, ctx, *at):
    c,x,y,z=slot_of(idx,dpi,ctx)
    @pl.when(c==0)
    def _(): pltpu.make_async_copy(src,keep.at[(x,y,z)+at],sem).start()
    @pl.when(c==1)
    def _(): pltpu.make_async_copy(src,send.at[(x,y,z)+at],sem).start()

def ffn_bwd_kernel(S, kind, first, idx, cb, h, wd, n2h, *refs):
    if not first:
        dn2in,*refs=refs
    gp=refs[:8]
    dn2, gk, gs, n2, gu_s, dh_s, act_s, dw_s, dd_s, sem, osem, nsem = refs[8:]
    q=pl.program_id(0)
    nq=4*S
    @pl.when(q==0)
    def _():
        load_rows(idx,kind,gp,gu_s,sem)
        if not first: pltpu.make_async_copy(dn2in,dn2,nsem.at[1]).start()
        pltpu.make_async_copy(n2h,n2,nsem.at[0]).start()
    wdq=wd[0]
    def grads(i):
        rows=slice(i*256,(i+1)*256)
        dact=dot(cb[rows,:],wdq,NT)
        parts=[];acts=[]
        for b in range(4):
            g=h[0,rows,b*2*S:b*2*S+S].astype(F32); u=h[0,rows,b*2*S+S:b*2*S+2*S].astype(F32)
            da=dact[:,b*S:(b+1)*S]
            sg=1/(1+jnp.exp(-g)); sl=g*sg
            acts.append((sl*u).astype(BF))
            parts.append((da*u*(sg+sl*(1-sg))).astype(BF)); parts.append((da*sl).astype(BF))
        dh_s[rows,:]=jnp.concatenate(parts,axis=-1); act_s[rows,:]=jnp.concatenate(acts,axis=-1)
    def back(i):
        rows=slice(i*256,(i+1)*256)
        t=dot(dh_s[rows,:],w,NT)
        dn2[rows,:]=(jnp.where(q==0,0.0,dn2[rows,:]) if first else dn2[rows,:])+t
    grads(0)
    wait_rows(gu_s,sem,q)
    @pl.when(q==0)
    def _():
        if not first: pltpu.make_async_copy(dn2in,dn2,nsem.at[1]).wait()
        pltpu.make_async_copy(n2h,n2,nsem.at[0]).wait()
    @pl.when(q==1)
    def _():
        pltpu.make_async_copy(dw_s.at[pl.ds(0,960)],dw_s.at[pl.ds(0,960)],osem.at[0]).wait()
        pltpu.make_async_copy(dd_s,dd_s,osem.at[1]).wait()
    for k in range(4): gu_s[4*q+k,960:1024,:]=jnp.zeros((64,2*S),BF)
    w=jnp.concatenate([gu_s[4*q+k] for k in range(4)],axis=-1)
    for i in range(1,4):
        back(i-1)
        grads(i)
    back(3)
    for m in range(nq//256):
        r=dot(act_s[:,m*256:(m+1)*256],cb[...],TN)
        for k in range(8):
            dd_s[k,m*256:(m+1)*256,:]=jnp.concatenate([r[:,k*120:(k+1)*120],jnp.zeros((256,8),F32)],axis=-1).astype(BF)
    for k in range(8):
        for cc in range(2):
            for t in range(2*S//128):
                put(idx,dd_s.at[k,pl.ds(cc*2*S+128*t,128)],gk,gs,osem.at[1],k,2*q+cc,pl.ds(240,128),pl.ds(128*t,128))
    def dw_step(m):
        cols=pl.ds(pl.multiple_of(m*256,256),256)
        dw_s[cols,:]=dot(n2[:,cols],dh_s[...],TN).astype(BF)
        return 0
    for m in range(4): dw_step(m)
    for b in range(4):
        for ctx in range(4):
            put(idx,dw_s.at[pl.ds(ctx*240,240),pl.ds(b*2*S,2*S)],gk,gs,osem.at[0],4*q+b,ctx,pl.ds(0,240))
    @pl.when(q==1)
    def _():
        pltpu.make_async_copy(dw_s.at[pl.ds(0,960)],dw_s.at[pl.ds(0,960)],osem.at[0]).wait()
        pltpu.make_async_copy(dd_s,dd_s,osem.at[1]).wait()

def ffn_bwd(idx, cb, n2, h, wd, dn2in, gp, kind, rows):
    S=gp[0].shape[2]//2
    full=const((T,DP))
    return pl.pallas_call(functools.partial(ffn_bwd_kernel,S,kind,dn2in is None), grid=(2,),
        in_specs=[SMEM,full,pl.BlockSpec((1,T,8*S),lambda q:(q,0,0)),pl.BlockSpec((1,4*S,DP),lambda q:(q,0,0))]+[ANY]*(9+(dn2in is not None)),
        out_specs=[full,ANY,ANY],
        out_shape=[sds((T,DP),F32)]+[sds((2,2,4,rows,2*S),BF)]*2,
        scratch_shapes=[pltpu.VMEM((T,DP),BF),pltpu.VMEM((8,DP,2*S),BF),pltpu.VMEM((T,8*S),BF),pltpu.VMEM((T,4*S),BF),pltpu.VMEM((DP,8*S),BF),pltpu.VMEM((8,4*S,128),BF)]+[pltpu.SemaphoreType.DMA((2,))]*3,
        compiler_params=params(), cost_estimate=cost(33), name="ffn_bwd")(idx,cb,h,wd,n2,*([] if dn2in is None else [dn2in]),*gp)

def block(f): return f.astype(F32)
def reduce_one_kernel(keep, rc, sx, sy, sxy):
    def s(x,y): return (block(keep[x,y,0])+block(rc[x,y,0])).astype(BF)
    sx[0]=s(1,0); sy[0]=s(0,1); sxy[0]=s(1,1)
def reduce_one(keep, rc):
    _,_,_,r,n=keep.shape
    b=pl.BlockSpec((2,2,1,r,n),lambda k:(0,0,k,0,0)); o=pl.BlockSpec((1,r,n),lambda k:(k,0,0))
    return pl.pallas_call(reduce_one_kernel,grid=(4,),in_specs=[b,b],out_specs=[o]*3,out_shape=[sds((4,r,n),BF)]*3,compiler_params=params(),cost_estimate=cost(3),name="reduce_one")(keep,rc)
def reduce_two_kernel(keep, rc, a, b, c, own, s1, s2, s3):
    k=pl.program_id(0)
    t=block(keep[0,0,0])+block(rc[0,0,0])+block(a[0])+block(b[0])+block(c[0])
    @pl.when(k==0)
    def _(): own[...]=t
    for j,s in ((1,s1),(2,s2),(3,s3)):
        @pl.when(k==j)
        def _(s=s): s[...]=t.astype(BF)
def reduce_two(keep, rc, a, b, c):
    _,_,_,r,n=keep.shape
    kb=pl.BlockSpec((1,1,1,r,n),lambda k:(0,0,k,0,0)); ib=pl.BlockSpec((1,r,n),lambda k:(k,0,0)); ob=pl.BlockSpec((r,n),lambda k:(0,0))
    return pl.pallas_call(reduce_two_kernel,grid=(4,),in_specs=[kb,kb,ib,ib,ib],out_specs=[ob]*4,out_shape=[sds((r,n),F32)]+[sds((r,n),BF)]*3,compiler_params=params(),cost_estimate=cost(3),name="reduce_two")(keep,rc,a,b,c)

NEG=-1e30
QB=256
def causal(keys, shape):
    a=lax.broadcasted_iota(jnp.int32,shape,keys); b=lax.broadcasted_iota(jnp.int32,shape,1-keys)%QB
    return a<=b

def attn_fwd_kernel(q, k, v, o, lse):
    n=3*QB
    for qi in range(T//QB):
        rows=slice(qi*QB,(qi+1)*QB); kn=(qi+1)*QB
        s=dot(q[:,rows,:].reshape(n,128),k[0,0:kn,:],NT)
        sd=jnp.where(causal(1,(n,QB)),s[:,kn-QB:],NEG)
        s=sd if qi==0 else jnp.concatenate([s[:,:kn-QB],sd],axis=-1)
        m=jnp.max(s,axis=-1,keepdims=True)
        r=dot(jnp.exp(s-m).astype(BF),v[0,0:kn,:])
        l=r[:,64:65]
        o[:,rows,:]=(r/l).astype(BF).reshape(3,QB,128)
        e=jnp.broadcast_to(m+jnp.log(l),(n,128)).T[0:1,:]
        for h in range(3): lse[h,:,rows]=e[:,h*QB:(h+1)*QB]

def attn_fwd(q,k,v,g0,ng):
    qs=pl.BlockSpec((3,T,128),lambda g:(g+g0,0,0)); ks=pl.BlockSpec((1,T,128),lambda g:(g+g0,0,0))
    return pl.pallas_call(attn_fwd_kernel,grid=(ng,),in_specs=[qs,ks,ks],
        out_specs=[pl.BlockSpec((3,T,128),lambda g:(g,0,0)),pl.BlockSpec((3,1,T),lambda g:(g,0,0))],
        out_shape=[sds((3*ng,T,128),BF),sds((3*ng,1,T),F32)],compiler_params=params(),cost_estimate=cost(6*ng),name="attn_fwd")(q,k,v)

def unrot(g,c,s,low):
    t=jnp.where(low,pltpu.roll(g,96,1),-pltpu.roll(g,32,1))
    return g*c+t*s

def attn_bwd_kernel(q,k,v,do,lse,delta,c,s,dq,dk,dv,dka,dva):
    n=3*QB
    low=lax.broadcasted_iota(jnp.int32,(QB,128),1)%64<32
    nb=T//QB
    for qi in range(nb-1,-1,-1):
        rows=slice(qi*QB,(qi+1)*QB); kn=(qi+1)*QB
        qb=q[:,rows,:].reshape(n,128); dob=do[:,rows,:].reshape(n,128); kb=k[0,0:kn,:]
        cat=lambda r: jnp.concatenate([r[h,:,rows] for h in range(3)],axis=-1)
        pt=jnp.exp(dot(kb,qb,NT)-cat(lse))
        pd=jnp.where(causal(0,(QB,n)),pt[kn-QB:],0.0)
        pt=pd if qi==0 else jnp.concatenate([pt[:kn-QB],pd],axis=0)
        dst=(pt*(dot(v[0,0:kn,:],dob,NT)-cat(delta))).astype(BF)
        a=dot(pt.astype(BF),dob); b=dot(dst,qb)
        if qi==nb-1: dva[...]=a; dka[...]=b
        else: dva[0:kn,:]+=a; dka[0:kn,:]+=b
        g=dot(dst,kb,TN)*0.125
        for h in range(3):
            dq[h,rows,:]=unrot(g[h*QB:(h+1)*QB],c[rows,:],s[rows,:],low).astype(BF)
    for qi in range(nb):
        rows=slice(qi*QB,(qi+1)*QB)
        dk[0,rows,:]=unrot(dka[rows,:],c[rows,:],s[rows,:],low).astype(BF)
        dv[0,rows,:]=dva[rows,:].astype(BF)

def attn_bwd(q,k,v,do,lse,delta,c,s,g0,ng):
    qs=pl.BlockSpec((3,T,128),lambda g:(g+g0,0,0)); ks=pl.BlockSpec((1,T,128),lambda g:(g+g0,0,0))
    qo=pl.BlockSpec((3,T,128),lambda g:(g,0,0)); ko=pl.BlockSpec((1,T,128),lambda g:(g,0,0))
    return pl.pallas_call(attn_bwd_kernel,grid=(ng,),in_specs=[qs,ks,ks,qs]+[pl.BlockSpec((3,1,T),lambda g:(g+g0,0,0))]*2+[const((T,128)),const((T,128))],
        out_specs=[qo,ko,ko],
        out_shape=[sds((3*ng,T,128),BF),sds((ng,T,128),BF),sds((ng,T,128),BF)],
        scratch_shapes=[pltpu.VMEM((T,128),F32),pltpu.VMEM((T,128),F32)],
        compiler_params=params(),cost_estimate=cost(9*ng),name="attn_bwd")(q,k,v,do,lse,delta,c,s)

EPS=1e-5
WN=1664
def prefetch(grid,in_specs,out_specs,scratch): return pltpu.PrefetchScalarGridSpec(num_scalar_prefetch=1,grid=grid,in_specs=in_specs,out_specs=out_specs,scratch_shapes=scratch)
def tok(i,idx): return (flip(i%2,idx[3]),flip(i//2,idx[2]),0,0)
tok_spec=lambda: pl.BlockSpec((1,1,D,256),tok)
row_spec=lambda n: pl.BlockSpec((256,n),lambda i,idx:(i,0))
head_spec=lambda h: pl.BlockSpec((h,256,128),lambda i,idx:(0,i,0))
def cst(shape): return pl.BlockSpec(shape,lambda *g:(0,)*len(shape))
def zeros(r,n,dt=F32): return jnp.zeros((r,n),dt)

def qkv_kernel(idx, x, c, s, *refs):
    pc=refs[:8]
    n1,q,k,v,w,gains,s1,sem=refs[8:]
    i=pl.program_id(0)
    @pl.when(i==0)
    def _():
        for src,dpi,ctx,_,_ in places(idx,"z",pc):
            pltpu.make_async_copy(src, s1.at[dpi,ctx], sem).start()
        pltpu.make_async_copy(s1,s1,sem).wait()
        for t in range(4):
            rows=slice(240*t,240*t+240)
            w[rows,:]=jnp.concatenate([s1[d,t,0:240,0:120] for d in range(8)]+[s1[d,t,0:240,128:168] for d in range(8)]+[s1[d,t,0:240,168:208] for d in range(8)]+[zeros(240,64,BF)],axis=-1)
        w[960:1024,:]=zeros(64,WN,BF)
        gl=[s1[d,t,240:256,0:128].astype(F32)[0:1,0:60] for d in range(8) for t in range(4)]
        gains[0:1,:]=jnp.concatenate(gl[:16]+[zeros(1,64)],axis=-1)
        gains[1:2,:]=jnp.concatenate(gl[16:]+[zeros(1,64)],axis=-1)
    xf=x[:,0:D].astype(F32)
    r=lax.rsqrt(jnp.sum(xf*xf,axis=-1,keepdims=True)*(1.0/D)+EPS)
    n=jnp.concatenate([(xf*r*gains[0:1,0:D]).astype(BF),zeros(256,64,BF)],axis=-1)
    n1[...]=n
    h=dot(n,w[...])
    low=lax.broadcasted_iota(jnp.int32,(256,128),1)%64<32
    z64=zeros(256,64,BF)
    one=jnp.where(lax.broadcasted_iota(jnp.int32,(256,64),1)==0,1.0,0.0).astype(BF)
    for t in range(10):
        g=h[:,128*t:128*t+128]
        u=jnp.where(low,-pltpu.roll(g,96,1),pltpu.roll(g,32,1))
        o=g*c[...]+u*s[...]
        for e in range(2):
            hd=2*t+e
            oh=o[:,64*e:64*e+64]
            if hd<15: q[hd]=jnp.concatenate([(oh*0.125).astype(BF),z64],axis=-1)
            else: k[hd-15]=jnp.concatenate([oh.astype(BF),z64],axis=-1)
    for e in range(5):
        v[e]=jnp.concatenate([h[:,1280+64*e:1344+64*e].astype(BF),one],axis=-1)

def qkv_fwd(idx,x,c,s,pc):
    return pl.pallas_call(qkv_kernel,grid_spec=prefetch((4,),[row_spec(DP),row_spec(128),row_spec(128)]+[ANY]*8,
        [row_spec(DP),head_spec(15),head_spec(5),head_spec(5),cst((DP,WN)),cst((2,DP))],
        [pltpu.VMEM((8,4,256,256),BF),pltpu.SemaphoreType.DMA]),
        out_shape=[sds((T,DP),BF),sds((15,T,128),BF),sds((5,T,128),BF),sds((5,T,128),BF),sds((DP,WN),BF),sds((2,DP),F32)],
        compiler_params=params(),cost_estimate=cost(16), name="qkv_fwd")(idx,x,c,s,*pc)

def out_kernel(idx,o1,o2,x,gains,*refs):
    pc=refs[:8]
    att,mid,n2,wo,ws,sem=refs[8:]
    @pl.when(pl.program_id(0)==0)
    def _():
        for src,dpi,ctx,_,_ in places(idx,"z",pc):
            for t in range(3):
                pltpu.make_async_copy(src.at[pl.ds(368,80),pl.ds(128*t,128)], ws.at[dpi,pl.ds(pl.multiple_of(ctx*240+80*t,16),80)], sem).start()
        pltpu.make_async_copy(ws,ws,sem).wait()
        wo[0:D,:]=jnp.concatenate([ws[d][:,0:120] for d in range(8)]+[zeros(D,64,BF)],axis=-1)
        wo[D:DP,:]=zeros(64,DP,BF)
    a=jnp.concatenate([o[h][:,0:64] for o in (o1,o2) for h in range(o.shape[0])]+[zeros(256,64,BF)],axis=-1)
    att[...]=a
    m=dot(a,wo[...])+x[...].astype(F32)
    mid[...]=m
    r=lax.rsqrt(jnp.sum(m*m,axis=-1,keepdims=True)*(1.0/D)+EPS)
    n2[...]=(m*r*gains[1:2,:]).astype(BF)

def out_fwd(idx,o1,o2,x,gains,pc):
    return pl.pallas_call(out_kernel,grid_spec=prefetch((4,),[head_spec(o1.shape[0]),head_spec(o2.shape[0]),row_spec(DP),cst((2,DP))]+[ANY]*8,
        [row_spec(DP)]*3+[cst((DP,DP))],[pltpu.VMEM((8,D,128),BF),pltpu.SemaphoreType.DMA]),out_shape=[sds((T,DP),BF),sds((T,DP),F32),sds((T,DP),BF),sds((DP,DP),BF)],compiler_params=params(),cost_estimate=cost(9),name="out_fwd")(idx,o1,o2,x,gains,*pc)

def tok_in_kernel(idx,h,r,g,o):
    y=idx[2]; c=idx[3]
    for ys,cs,v in ((0,0,h[2*y+c]),(1,0,r[c]),(0,1,g[0]),(1,1,g[1])):
        b=2*flip(y,ys)+flip(c,cs)
        o[pl.ds(pl.multiple_of(256*b,256),256),:]=jnp.concatenate([v,zeros(64,256,BF)],axis=0).T
def tok_in(idx,h,r,g):
    return pl.pallas_call(tok_in_kernel,in_specs=[SMEM]+[pl.BlockSpec(memory_space=pltpu.VMEM)]*3,out_specs=pl.BlockSpec(memory_space=pltpu.VMEM),out_shape=sds((T,DP),BF),compiler_params=params(),cost_estimate=cost(4),name="tok_in")(idx,h,r,g)

def out_bwd_kernel(idx,dn2,cb,mid,gains,wo,att,kin,sin,dmid,do,dg,ok,os_,delta,dbr_s,st,sem):
    i=pl.program_id(0)
    rows=pl.ds(pl.multiple_of(i*256,256),256)
    m=mid[...]; r=lax.rsqrt(jnp.sum(m*m,axis=-1,keepdims=True)*(1.0/D)+EPS)
    d=dn2[...]; gd=gains[1:2,:]*d
    dm=cb[...].astype(F32)+r*gd-m*(r*r*r)*(jnp.sum(gd*m,axis=-1,keepdims=True)*(1.0/D))
    dmid[...]=dm
    g=jnp.sum(d*m*r,axis=0,keepdims=True)
    dg[...]=g+jnp.where(i==0,0.0,dg[...])
    b=dm.astype(BF)
    dbr_s[rows,:]=b
    da=dot(b,wo[...],NT).astype(BF)
    z64=zeros(256,64,BF)
    for h in range(15): do[h]=jnp.concatenate([da[:,64*h:64*h+64],z64],axis=-1)
    p=da.astype(F32)*att[rows,:].astype(F32)
    hi=p.astype(BF); lo=(p-hi.astype(F32)).astype(BF)
    e=jnp.where(lax.broadcasted_iota(jnp.int32,(DP,128),0)//64==lax.broadcasted_iota(jnp.int32,(DP,128),1),1.0,0.0).astype(BF)
    de=(dot(hi,e)+dot(lo,e)).T
    for h in range(15): delta[h]=de[h:h+1,:]
    @pl.when(i==3)
    def _():
        for mm in range(4):
            rr=dot(att[:,256*mm:256*mm+256],dbr_s[...],TN)
            for k in range(8):
                st[k,256*mm:256*mm+256,:]=jnp.concatenate([rr[:,120*k:120*k+120],zeros(256,8)],axis=-1).astype(BF)
        for k in range(8):
            for t in range(4):
                put(idx,st.at[k,pl.ds(240*t,128)],ok,os_,sem,k,t,pl.ds(368,128),pl.ds(0,128)); put(idx,st.at[k,pl.ds(240*t+128,112)],ok,os_,sem,k,t,pl.ds(368,112),pl.ds(128,128))
        pltpu.make_async_copy(st.at[:,pl.ds(0,960)],st.at[:,pl.ds(0,960)],sem).wait()

def out_bwd(idx,dn2,cb,mid,gains,wo,att,keep,send):
    return pl.pallas_call(out_bwd_kernel,grid_spec=prefetch((4,),[row_spec(DP)]*3+[cst((2,DP)),cst((DP,DP)),cst((T,DP)),ANY,ANY],
        [row_spec(DP),head_spec(15),cst((1,DP)),ANY,ANY,pl.BlockSpec((15,1,256),lambda i,idx:(0,0,i))],[pltpu.VMEM((T,DP),BF),pltpu.VMEM((8,DP,128),BF),pltpu.SemaphoreType.DMA]),
        out_shape=[sds((T,DP),F32),sds((15,T,128),BF),sds((1,DP),F32)]+[sds(keep.shape,BF)]*2+[sds((15,1,T),F32)],input_output_aliases={7:3,8:4},
        compiler_params=params(),cost_estimate=cost(16), name="out_bwd")(idx,dn2,cb,mid,gains,wo,att,keep,send)

def qkv_dx_kernel(idx,dq1,dk1,dv1,dq2,dk2,dv2,dq3,dk3,dv3,x,gains,dmid,w,hg,dh,dg1):
    i=pl.program_id(0)
    h=jnp.concatenate([r[h][:,0:64] for r in (dq1,dq2,dq3,dk1,dk2,dk3,dv1,dv2,dv3) for h in range(r.shape[0])]+[zeros(256,64,BF)],axis=-1)
    dh[...]=h
    d=dot(h,w[...],NT)
    xf=x[...].astype(F32)
    r=lax.rsqrt(jnp.sum(xf*xf,axis=-1,keepdims=True)*(1.0/D)+EPS)
    gd=gains[0:1,:]*d
    hh=dmid[...]+r*gd-xf*(r*r*r)*(jnp.sum(gd*xf,axis=-1,keepdims=True)*(1.0/D))
    hg[0,0]=hh.T[:D,:].astype(BF)
    g=jnp.sum(d*xf*r,axis=0,keepdims=True)
    dg1[...]=g+jnp.where(i==0,0.0,dg1[...])

def qkv_dx(idx,g1,g2,g3,x,gains,dmid,w):
    return pl.pallas_call(qkv_dx_kernel,grid_spec=prefetch((4,),[head_spec(a.shape[0]) for a in (*g1,*g2,*g3)]+[row_spec(DP),cst((2,DP)),row_spec(DP),cst((DP,WN))],
        [tok_spec(),row_spec(WN),cst((1,DP))],[]),out_shape=[sds((2,2,D,256),BF),sds((T,WN),BF),sds((1,DP),F32)],
        compiler_params=params(),cost_estimate=cost(9),name="qkv_dx")(idx,*g1,*g2,*g3,x,gains,dmid,w)

def qkv_dw_kernel(idx,n1,dh,dg1,dg2,wk,ws,st,sg,sem):
    m=pl.program_id(0)
    r=dot(n1[...],dh[...],TN)
    rows=pl.ds(pl.multiple_of(256*m,256),256)
    for k in range(8):
        st[k,rows,:]=jnp.concatenate([r[:,120*k:120*k+120],zeros(256,8),r[:,960+40*k:1000+40*k],r[:,1280+40*k:1320+40*k],zeros(256,48)],axis=-1).astype(BF)
    @pl.when(m==3)
    def _():
        sg[...]=jnp.zeros_like(sg)
        for k in range(8):
            for t in range(4):
                o=(4*k+t)*60
                src=dg1[:,o:o+60] if k<4 else dg2[:,o-960:o-900]
                sg[k,t,:,0:128]=jnp.broadcast_to(jnp.concatenate([src,zeros(1,68)],axis=-1),(16,128)).astype(BF)
                put(idx,st.at[k,pl.ds(240*t,240)],wk,ws,sem,k,t,pl.ds(0,240))
                put(idx,sg.at[k,t],wk,ws,sem,k,t,pl.ds(240,16))
        pltpu.make_async_copy(st.at[:,pl.ds(0,960)],st.at[:,pl.ds(0,960)],sem).wait()
        pltpu.make_async_copy(sg,sg,sem).wait()

def qkv_dw(idx,n1,dh,dg1,dg2):
    return pl.pallas_call(qkv_dw_kernel,grid_spec=prefetch((4,),[pl.BlockSpec((T,256),lambda m,idx:(0,m)),cst((T,WN)),cst((1,DP)),cst((1,DP))],
        [ANY,ANY],[pltpu.VMEM((8,DP,256),BF),pltpu.VMEM((8,4,16,256),BF),pltpu.SemaphoreType.DMA]),out_shape=[sds((2,2,4,256,256),BF)]*2,
        compiler_params=params(),cost_estimate=cost(9),name="qkv_dw")(idx,n1,dh,dg1,dg2)

def tok_out_kernel(idx,a,r,b,o):
    y=idx[2]; c=idx[3]
    o[2*y+c]=a[0,0]; o[2*y+1-c]=r[0]
    o[2*(1-y)+c]=b[0]; o[2*(1-y)+1-c]=b[1]
def tok_out(idx,a,r,b):
    v=pl.BlockSpec(memory_space=pltpu.VMEM)
    return pl.pallas_call(tok_out_kernel,grid=(1,),in_specs=[SMEM,pl.BlockSpec((1,1,D,256),lambda i:(0,0,0,0)),pl.BlockSpec((1,D,256),lambda i:(0,0,0)),v],out_specs=v,out_shape=sds((4,D,256),BF),compiler_params=params(),cost_estimate=cost(4),name="tok_out")(idx,a,r,b)


def swap(a, axis, bit):
    n = lax.axis_size(axis)
    return lax.ppermute(a, axis, [(i, i ^ bit) for i in range(n)])

def move(a, name):
    if name == "xy":
        n = lax.axis_size("ctx")
        return lax.ppermute(a, ("dp", "ctx"), [(i, (i // n ^ 1) * n + (i % n ^ 2)) for i in range(n * lax.axis_size("dp"))])
    if name == "x": return swap(a, "dp", 1)
    if name == "y": return swap(a, "ctx", 2)
    return swap(a, "ctx", 1)

def from_z(a, k):
    return lax.ppermute(a, "dp", [(((z + k) % 4) * 2 + x, z * 2 + x) for z in range(4) for x in range(2)])

def after(a, *others):
    return lax.optimization_barrier((a,) + others)[0]

def gather_z(shard):
    return jnp.stack([shard] + [from_z(shard, k) for k in (1, 2, 3)])

def gather_rest(g):
    ps = [g] + [move(g, name) for name in ("y", "x", "xy")]
    return ps + [move(p, "c") for p in ps]

def gather_flat(shard):
    g = jnp.stack([shard] + [move(shard, name) for name in ("y", "x", "xy")])
    ps = [g] + [from_z(g, k) for k in (1, 2, 3)]
    return ps + [move(p, "c") for p in ps]

def add(*terms):
    total = terms[0].astype(F32)
    for t in terms[1:]: total = total + t.astype(F32)
    return total

def reduce_pieces(keep, send):
    rc = move(send, "c")
    parts = reduce_one(keep, rc)
    parts = [move(p, n) for p, n in zip(parts, ("x", "y", "xy"))]
    own, *rest = reduce_two(keep, rc, *parts)
    return add(own, *[from_z(p, 3 - k) for k, p in enumerate(rest)])

def exchange_in_y(idx, a):
    return move(lax.dynamic_slice_in_dim(a, 2 * (1 - idx[2]), 2, 0), "y")

def exchange_in_c(idx, a, r):
    y, c = idx[2], idx[3]
    give = jnp.concatenate([lax.dynamic_slice_in_dim(a, 2 * y + 1 - c, 1, 0), lax.dynamic_slice_in_dim(r, 1 - c, 1, 0)])
    return move(give, "c")

SPLIT = ((0, 192), (192, 320))

def fast(hidden_in, norm_gains, w_query, w_key, w_value, w_out, w_gate, w_up, w_down, cotangent):
    di, ci = lax.axis_index("dp"), lax.axis_index("ctx")
    idx = jnp.stack([di // 2, di % 2, ci // 2, ci % 2]).astype(jnp.int32)
    pz = lambda r, n: jnp.zeros((r, n), BF)
    c1 = jnp.concatenate([w_query, pz(240, 8), w_key, w_value, pz(240, 48)], axis=1)
    gain_row = jnp.pad(norm_gains.reshape(1, 60), ((0, 15), (0, 196)))
    c1 = jnp.concatenate([c1, gain_row], axis=0)
    def pack(lo, hi):
        s = hi - lo
        gu = jnp.concatenate([w_gate[:, lo:hi], w_up[:, lo:hi]], axis=1)
        d = jnp.concatenate([w_down[lo:hi], w_down[320 + lo:320 + hi]], axis=0)
        d = jnp.pad(d, ((0, 0), (0, 8)))
        d = jnp.concatenate([d[128 * t:128 * t + 128] for t in range(2 * s // 128)], axis=1)
        return jnp.concatenate([gu, d], axis=0)
    wo = jnp.pad(w_out, ((0, 0), (0, 8)))
    wo = jnp.concatenate([wo[80 * t:80 * t + 80] for t in range(3)], axis=1)
    ht, ct = jnp.swapaxes(hidden_in, 1, 2), jnp.swapaxes(cotangent, 1, 2)
    xr = exchange_in_y(idx, ht)
    g1 = gather_z(c1)
    ga = gather_z(jnp.concatenate([pack(*SPLIT[0]), wo], axis=0))
    p1 = gather_rest(g1)
    xr = after(xr, p1[1])
    xg = exchange_in_c(idx, ht, xr)
    x = tok_in(idx, ht, xr, xg)
    pa = gather_rest(ga)
    pb = gather_flat(pack(*SPLIT[1]))
    cr = exchange_in_y(idx, ct)
    cg = exchange_in_c(idx, ct, cr)
    cos, sin = rope_tables(jnp.arange(T).astype(F32), HD)
    cos, sin = jnp.tile(cos, (1, 2)), jnp.tile(sin, (1, 2))
    n1, q, k, v, w, gains = qkv_fwd(idx, x, cos, sin, p1)
    o1, lse1 = attn_fwd(q, k, v, 0, 3)
    o2, lse2 = attn_fwd(q, k, v, 3, 2)
    att, mid, n2, wo = out_fwd(idx, o1, o2, x, gains, pa)
    acc, ha, wda = ffn_fwd(idx, n2, mid, pa, "z", False)
    out, hb, wdb = ffn_fwd(idx, n2, acc, pb, "xy", True)
    cb = tok_in(idx, ct, cr, cg)
    hr = move(out[1], "c")
    hb_ = move(jnp.stack([out[0, 1], hr[1]]), "y")
    hidden_out = tok_out(idx, out, hr, hb_)
    dn2, ka, sa = ffn_bwd(idx, cb, n2, ha, wda, None, pa, "z", 368)
    dn2, kb, sb = ffn_bwd(idx, cb, n2, hb, wdb, dn2, pb, "xy", 496)
    dmid, do, dg2, kb, sb, delta = out_bwd(idx, dn2, cb, mid, gains, wo, att, kb, sb)
    lse = jnp.concatenate([lse1, lse2], axis=0)
    b1 = attn_bwd(q, k, v, do, lse, delta, cos, sin, 0, 1)
    b2 = attn_bwd(q, k, v, do, lse, delta, cos, sin, 1, 2)
    b3 = attn_bwd(q, k, v, do, lse, delta, cos, sin, 3, 2)
    hg, dh, dg1 = qkv_dx(idx, b1, b2, b3, x, gains, dmid, w)
    kq, sq = qkv_dw(idx, n1, dh, dg1, dg2)
    gr = move(hg[1], "c")
    gb_ = move(jnp.stack([hg[0, 1], gr[1]]), "y")
    hidden_grad = tok_out(idx, hg, gr, gb_)
    factor = 1.0 / math.sqrt(lax.axis_size("dp") * hidden_in.shape[0] * T)
    ra = reduce_pieces(ka, sa) * factor
    rb = reduce_pieces(kb, sb) * factor
    rq = reduce_pieces(kq, sq) * factor
    ro = jnp.concatenate([rb[368:496, :120], rb[368:480, 128:248]], axis=0)
    gate, up, down = [], [], []
    for (lo, hi), r in zip(SPLIT, (ra, rb)):
        s = hi - lo
        gate.append(r[:240, :s]); up.append(r[:240, s:])
        d = jnp.concatenate([r[240:368, 128 * t:128 * t + 128] for t in range(2 * s // 128)], axis=0)[:, :120]
        down.append((d[:s], d[s:]))
    return (jnp.swapaxes(hidden_out, 1, 2), jnp.swapaxes(hidden_grad, 1, 2), rq[240, :60], rq[:240, :120], rq[:240, 128:168],
            rq[:240, 168:208], ro, jnp.concatenate(gate, axis=1), jnp.concatenate(up, axis=1),
            jnp.concatenate([down[0][0], down[1][0], down[0][1], down[1][1]], axis=0))


def body(hidden_in, *rest):
    seqs_here, seg_len, _ = hidden_in.shape
    if (lax.axis_size("dp"), lax.axis_size("ctx"), seqs_here, seg_len) == (8, 4, 4, 256):
        return fast(hidden_in, *rest)
    return local(hidden_in, *rest)


def solution(mesh):
    in_specs = (
        P("dp", "ctx", None),
        P(("dp", "ctx")),
        P("ctx", "dp"),
        P("ctx", "dp"),
        P("ctx", "dp"),
        P("ctx", "dp"),
        P("ctx", "dp"),
        P("ctx", "dp"),
        P("ctx", "dp"),
        P("dp", "ctx", None),
    )
    out_specs = (
        P("dp", "ctx", None),
        P("dp", "ctx", None),
        P(("dp", "ctx")),
        P("ctx", "dp"),
        P("ctx", "dp"),
        P("ctx", "dp"),
        P("ctx", "dp"),
        P("ctx", "dp"),
        P("ctx", "dp"),
        P("ctx", "dp"),
    )
    return jax.shard_map(body, mesh=mesh, in_specs=in_specs, out_specs=out_specs, check_vma=False)
```

```python
import functools
import math

import jax
import jax.numpy as jnp
from jax import lax
from jax.experimental import pallas as pl
from jax.experimental.pallas import tpu as pltpu
from jax.sharding import PartitionSpec as P


QH = 15
KVH = 5
HD = 64


epsilon = 1e-05
rope_base = 100000.0
masked_score = -1e30
contract_last = (((1,), (1,)), ((), ()))
contract_first = (((0,), (0,)), ((), ()))


def rope_tables(positions, head_size):
    half_size = head_size // 2
    frequencies = jnp.exp(
        -(jnp.arange(half_size).astype(jnp.float32) * (2.0 / head_size)) * math.log(rope_base)
    )
    angles = positions[:, None] * frequencies[None, :]
    angles = jnp.concatenate([angles, angles], axis=-1)
    return (jnp.cos(angles), jnp.sin(angles))


def rotate(values, cos_table, sin_table):
    half_size = values.shape[-1] // 2
    turned = jnp.concatenate([-values[..., half_size:], values[..., :half_size]], axis=-1)
    return values * cos_table[:, None, :] + turned * sin_table[:, None, :]


def unrotate(grad_turned, cos_table, sin_table):
    _, pullback = jax.vjp(lambda values: rotate(values, cos_table, sin_table), grad_turned)
    return pullback(grad_turned)[0]


def rms_scale(values, gain_row):
    return (
        values * lax.rsqrt(jnp.mean(values * values, axis=-1, keepdims=True) + epsilon) * gain_row
    )


def local(hidden_in, norm_gains, w_query, w_key, w_value, w_out, w_gate, w_up, w_down, cotangent):
    seqs_here, seg_len, model_width = hidden_in.shape
    ctx_size = lax.axis_size("ctx")
    dp_size = lax.axis_size("dp")
    full_len = seg_len * ctx_size
    rows_here = seqs_here * seg_len
    per_group = QH // KVH
    score_scale = HD ** (-0.5)
    row_parts = (
        lax.all_gather(w_query, "ctx", axis=0, tiled=True),
        lax.all_gather(w_key, "ctx", axis=0, tiled=True),
        lax.all_gather(w_value, "ctx", axis=0, tiled=True),
        lax.all_gather(w_out, "ctx", axis=0, tiled=True),
        lax.all_gather(w_gate, "ctx", axis=0, tiled=True),
        lax.all_gather(w_up, "ctx", axis=0, tiled=True),
        lax.all_gather(w_down, "ctx", axis=0, tiled=True),
        lax.all_gather(norm_gains.reshape(-1, 1), "ctx", axis=0, tiled=True),
    )
    gathered = (
        lax.all_gather(row_parts[0], "dp", axis=1, tiled=True),
        lax.all_gather(row_parts[1], "dp", axis=1, tiled=True),
        lax.all_gather(row_parts[2], "dp", axis=1, tiled=True),
        lax.all_gather(row_parts[3], "dp", axis=1, tiled=True),
        lax.all_gather(row_parts[4], "dp", axis=1, tiled=True),
        lax.all_gather(row_parts[5], "dp", axis=1, tiled=True),
        lax.all_gather(row_parts[6], "dp", axis=1, tiled=True),
        lax.all_gather(row_parts[7].reshape(1, -1), "dp", axis=1, tiled=True),
    )
    first_pos = lax.axis_index("ctx") * seg_len + jnp.arange(seg_len)
    cos_table, sin_table = rope_tables(first_pos.astype(jnp.float32), HD)
    row_pos = jnp.tile(first_pos, per_group)
    causal_mask = jnp.arange(full_len)[None, :] <= row_pos[:, None]

    def group_queries(tensor):
        return (
            tensor.reshape(seqs_here, seg_len, KVH, per_group, HD)
            .transpose(0, 2, 3, 1, 4)
            .reshape(seqs_here * KVH, per_group * seg_len, HD)
        )

    def ungroup_queries(tensor):
        return (
            tensor.reshape(seqs_here, KVH, per_group, seg_len, HD)
            .transpose(0, 3, 1, 2, 4)
            .reshape(rows_here, QH * HD)
        )

    def group_keys(tensor):
        return (
            tensor.reshape(seqs_here, full_len, KVH, HD)
            .transpose(0, 2, 1, 3)
            .reshape(seqs_here * KVH, full_len, HD)
        )

    def ungroup_keys(tensor):
        return (
            tensor.reshape(seqs_here, KVH, full_len, HD)
            .transpose(0, 2, 1, 3)
            .reshape(seqs_here, full_len, KVH * HD)
        )

    def block_scores(query_block, key_block):
        raw_scores = (
            lax.dot_general(
                query_block, key_block, contract_last, preferred_element_type=jnp.float32
            )
            * score_scale
        )
        return jnp.where(causal_mask, raw_scores, masked_score)

    def attend_forward(triple):
        query_block, key_block, value_block = triple
        scores = block_scores(query_block, key_block)
        row_top = jnp.max(scores, axis=-1, keepdims=True)
        exponents = jnp.exp(scores - row_top)
        totals = jnp.sum(exponents, axis=-1, keepdims=True)
        attn_weights = exponents / totals
        attended = jnp.dot(
            attn_weights.astype(jnp.bfloat16), value_block, preferred_element_type=jnp.float32
        )
        return (attended, (row_top + jnp.log(totals))[:, 0])

    gains_full = gathered[7].reshape(-1).astype(jnp.float32)
    inputs_f32 = hidden_in.reshape(rows_here, model_width).astype(jnp.float32)
    normed = rms_scale(inputs_f32, gains_full[:model_width]).astype(jnp.bfloat16)
    queries = jnp.dot(normed, gathered[0], preferred_element_type=jnp.float32).reshape(
        seqs_here, seg_len, QH, HD
    )
    key_proj = jnp.dot(normed, gathered[1], preferred_element_type=jnp.float32).reshape(
        seqs_here, seg_len, KVH, HD
    )
    value_proj = (
        jnp.dot(normed, gathered[2], preferred_element_type=jnp.float32)
        .astype(jnp.bfloat16)
        .reshape(seqs_here, seg_len, KVH * HD)
    )
    turned_query = rotate(queries, cos_table, sin_table).astype(jnp.bfloat16)
    turned_key = (
        rotate(key_proj, cos_table, sin_table)
        .astype(jnp.bfloat16)
        .reshape(seqs_here, seg_len, KVH * HD)
    )
    key_sets = (
        lax.all_gather(turned_key, "ctx", axis=1, tiled=True),
        lax.all_gather(value_proj, "ctx", axis=1, tiled=True),
    )
    grouped_query = group_queries(turned_query)
    attended, log_totals = lax.map(
        attend_forward, (grouped_query, group_keys(key_sets[0]), group_keys(key_sets[1]))
    )
    mixed_heads = ungroup_queries(attended).astype(jnp.bfloat16)
    middle = inputs_f32 + jnp.dot(mixed_heads, gathered[3], preferred_element_type=jnp.float32)
    normed_two = rms_scale(middle, gains_full[model_width:]).astype(jnp.bfloat16)
    gate_pre = jnp.dot(normed_two, gathered[4], preferred_element_type=jnp.float32)
    up_pre = jnp.dot(normed_two, gathered[5], preferred_element_type=jnp.float32)
    product = (jax.nn.silu(gate_pre) * up_pre).astype(jnp.bfloat16)
    result = middle + jnp.dot(product, gathered[6], preferred_element_type=jnp.float32)
    hidden_out = result.astype(jnp.bfloat16).reshape(seqs_here, seg_len, model_width)
    rows_again = (
        lax.all_gather(w_query, "ctx", axis=0, tiled=True),
        lax.all_gather(w_key, "ctx", axis=0, tiled=True),
        lax.all_gather(w_value, "ctx", axis=0, tiled=True),
        lax.all_gather(w_out, "ctx", axis=0, tiled=True),
        lax.all_gather(w_gate, "ctx", axis=0, tiled=True),
        lax.all_gather(w_up, "ctx", axis=0, tiled=True),
        lax.all_gather(w_down, "ctx", axis=0, tiled=True),
        lax.all_gather(norm_gains.reshape(-1, 1), "ctx", axis=0, tiled=True),
    )
    refetched = (
        lax.all_gather(rows_again[0], "dp", axis=1, tiled=True),
        lax.all_gather(rows_again[1], "dp", axis=1, tiled=True),
        lax.all_gather(rows_again[2], "dp", axis=1, tiled=True),
        lax.all_gather(rows_again[3], "dp", axis=1, tiled=True),
        lax.all_gather(rows_again[4], "dp", axis=1, tiled=True),
        lax.all_gather(rows_again[5], "dp", axis=1, tiled=True),
        lax.all_gather(rows_again[6], "dp", axis=1, tiled=True),
        lax.all_gather(rows_again[7].reshape(1, -1), "dp", axis=1, tiled=True),
    )
    keys_again = (
        lax.all_gather(turned_key, "ctx", axis=1, tiled=True),
        lax.all_gather(value_proj, "ctx", axis=1, tiled=True),
    )
    gains_back = refetched[7].reshape(-1).astype(jnp.float32)
    seed_low = cotangent.reshape(rows_here, model_width)
    seed_high = seed_low.astype(jnp.float32)
    down_part = lax.dot_general(
        product, seed_low, contract_first, preferred_element_type=jnp.float32
    )
    grad_product = lax.dot_general(
        seed_low, refetched[6], contract_last, preferred_element_type=jnp.float32
    )
    _, gate_pull = jax.vjp(
        lambda gate_in, up_in: jax.nn.silu(gate_in) * up_in, gate_pre, up_pre
    )
    grad_gate, grad_up = gate_pull(grad_product)
    grad_gate = grad_gate.astype(jnp.bfloat16)
    grad_up = grad_up.astype(jnp.bfloat16)
    gate_part = lax.dot_general(
        normed_two, grad_gate, contract_first, preferred_element_type=jnp.float32
    )
    up_part = lax.dot_general(
        normed_two, grad_up, contract_first, preferred_element_type=jnp.float32
    )
    grad_normed_two = lax.dot_general(
        grad_gate, refetched[4], contract_last, preferred_element_type=jnp.float32
    ) + lax.dot_general(grad_up, refetched[5], contract_last, preferred_element_type=jnp.float32)
    _, second_pull = jax.vjp(rms_scale, middle, gains_back[model_width:])
    grad_middle_norm, gain_two_part = second_pull(grad_normed_two)
    grad_middle = seed_high + grad_middle_norm
    grad_branch = grad_middle.astype(jnp.bfloat16)
    out_part = lax.dot_general(
        mixed_heads, grad_branch, contract_first, preferred_element_type=jnp.float32
    )
    grad_mixed = lax.dot_general(
        grad_branch, refetched[3], contract_last, preferred_element_type=jnp.float32
    ).astype(jnp.bfloat16)

    def attend_backward(bundle):
        query_block, key_block, value_block, log_total, grad_block = bundle
        scores = block_scores(query_block, key_block)
        attn_weights = jnp.exp(scores - log_total[:, None])
        grad_weights = lax.dot_general(
            grad_block, value_block, contract_last, preferred_element_type=jnp.float32
        )
        grad_values = lax.dot_general(
            attn_weights.astype(jnp.bfloat16),
            grad_block,
            contract_first,
            preferred_element_type=jnp.float32,
        )
        grad_scores = (
            attn_weights
            * (grad_weights - jnp.sum(attn_weights * grad_weights, axis=-1, keepdims=True))
        ).astype(jnp.bfloat16)
        grad_queries = (
            jnp.dot(grad_scores, key_block, preferred_element_type=jnp.float32) * score_scale
        )
        grad_keys = (
            lax.dot_general(
                grad_scores, query_block, contract_first, preferred_element_type=jnp.float32
            )
            * score_scale
        )
        return (grad_queries, grad_keys, grad_values)

    grad_grouped = group_queries(grad_mixed.reshape(seqs_here, seg_len, QH, HD))
    query_blocks, key_blocks, value_blocks = lax.map(
        attend_backward,
        (
            grouped_query,
            group_keys(keys_again[0]),
            group_keys(keys_again[1]),
            log_totals,
            grad_grouped,
        ),
    )
    key_sums = (
        lax.psum_scatter(ungroup_keys(key_blocks), "ctx", scatter_dimension=1, tiled=True),
        lax.psum_scatter(ungroup_keys(value_blocks), "ctx", scatter_dimension=1, tiled=True),
    )
    grad_query = (
        unrotate(
            ungroup_queries(query_blocks).reshape(seqs_here, seg_len, QH, HD), cos_table, sin_table
        )
        .astype(jnp.bfloat16)
        .reshape(rows_here, QH * HD)
    )
    grad_key = (
        unrotate(key_sums[0].reshape(seqs_here, seg_len, KVH, HD), cos_table, sin_table)
        .astype(jnp.bfloat16)
        .reshape(rows_here, KVH * HD)
    )
    grad_value = key_sums[1].astype(jnp.bfloat16).reshape(rows_here, KVH * HD)
    query_part = lax.dot_general(
        normed, grad_query, contract_first, preferred_element_type=jnp.float32
    )
    key_part = lax.dot_general(normed, grad_key, contract_first, preferred_element_type=jnp.float32)
    value_part = lax.dot_general(
        normed, grad_value, contract_first, preferred_element_type=jnp.float32
    )
    grad_normed = (
        lax.dot_general(grad_query, refetched[0], contract_last, preferred_element_type=jnp.float32)
        + lax.dot_general(grad_key, refetched[1], contract_last, preferred_element_type=jnp.float32)
        + lax.dot_general(
            grad_value, refetched[2], contract_last, preferred_element_type=jnp.float32
        )
    )
    _, first_pull = jax.vjp(rms_scale, inputs_f32, gains_back[:model_width])
    grad_inputs_norm, gain_one_part = first_pull(grad_normed)
    hidden_grad = (
        (grad_middle + grad_inputs_norm)
        .astype(jnp.bfloat16)
        .reshape(seqs_here, seg_len, model_width)
    )
    gain_part = jnp.concatenate([gain_one_part, gain_two_part])
    col_sums = (
        lax.psum_scatter(query_part, "dp", scatter_dimension=1, tiled=True),
        lax.psum_scatter(key_part, "dp", scatter_dimension=1, tiled=True),
        lax.psum_scatter(value_part, "dp", scatter_dimension=1, tiled=True),
        lax.psum_scatter(out_part, "dp", scatter_dimension=1, tiled=True),
        lax.psum_scatter(gate_part, "dp", scatter_dimension=1, tiled=True),
        lax.psum_scatter(up_part, "dp", scatter_dimension=1, tiled=True),
        lax.psum_scatter(down_part, "dp", scatter_dimension=1, tiled=True),
        lax.psum_scatter(gain_part.reshape(1, -1), "dp", scatter_dimension=1, tiled=True),
    )
    owned = (
        lax.psum_scatter(col_sums[0], "ctx", scatter_dimension=0, tiled=True),
        lax.psum_scatter(col_sums[1], "ctx", scatter_dimension=0, tiled=True),
        lax.psum_scatter(col_sums[2], "ctx", scatter_dimension=0, tiled=True),
        lax.psum_scatter(col_sums[3], "ctx", scatter_dimension=0, tiled=True),
        lax.psum_scatter(col_sums[4], "ctx", scatter_dimension=0, tiled=True),
        lax.psum_scatter(col_sums[5], "ctx", scatter_dimension=0, tiled=True),
        lax.psum_scatter(col_sums[6], "ctx", scatter_dimension=0, tiled=True),
        lax.psum_scatter(col_sums[7].reshape(-1, 1), "ctx", scatter_dimension=0, tiled=True),
    )
    factor = 1.0 / math.sqrt(dp_size * seqs_here * full_len)
    return (
        hidden_out,
        hidden_grad,
        owned[7].reshape(-1) * factor,
        owned[0] * factor,
        owned[1] * factor,
        owned[2] * factor,
        owned[3] * factor,
        owned[4] * factor,
        owned[5] * factor,
        owned[6] * factor,
    )


BF=jnp.bfloat16; F32=jnp.float32
T=1024; D=960; DP=1024
NT=(((1,),(1,)),((),())); NN=(((1,),(0,)),((),())); TN=(((0,),(0,)),((),()))
def dot(a,b,dn=NN): return lax.dot_general(a,b,dn,preferred_element_type=F32)
ANY=pl.BlockSpec(memory_space=pltpu.HBM)
SMEM=pl.BlockSpec(memory_space=pltpu.SMEM)
def flip(a,b): return lax.bitwise_xor(a,b)
def const(shape): return pl.BlockSpec(shape,lambda *g:(0,)*len(shape))
def params(mib): return pltpu.CompilerParams(vmem_limit_bytes=mib<<20)
def cost(us): return pl.CostEstimate(flops=int(us*9e8),bytes_accessed=int(us*2e6),transcendentals=0)
def sds(shape,dt): return jax.ShapeDtypeStruct(shape,dt)

def places(idx, kind, pieces):
    for dc in range(2):
        for dx in range(2):
            for dy in range(2):
                for dz in range(4):
                    src=pieces[4*dc+2*dx+dy].at[dz] if kind=="z" else pieces[4*dc+dz].at[2*dx+dy]
                    z=lax.rem(idx[0]+dz,4); y=flip(idx[2],dy)
                    yield src, 2*z+flip(idx[1],dx), 2*y+flip(idx[3],dc), z, y

def load_rows(idx, kind, pieces, dst, sem):
    for src,dpi,ctx,z,_ in places(idx,kind,pieces):
        pltpu.make_async_copy(src.at[pl.ds(0,240)], dst.at[dpi,pl.ds(pl.multiple_of(ctx*240,16),240)], sem.at[z//2]).start()

def wait_rows(dst, sem, j):
    half=dst.at[pl.ds(4*j,4),pl.ds(0,960)]
    pltpu.make_async_copy(half,half,sem.at[j]).wait()

def load_cols(idx, kind, pieces, dst, sem):
    for src,dpi,ctx,_,y in places(idx,kind,pieces):
        for t in range(dst.shape[2]//128):
            pltpu.make_async_copy(src.at[pl.ds(240,128),pl.ds(128*t,128)], dst.at[ctx,dpi,pl.ds(128*t,128)], sem.at[y]).start()

def wait_cols(dst, sem, j):
    half=dst.at[pl.ds(2*j,2)]
    pltpu.make_async_copy(half,half,sem.at[j]).wait()

def ffn_fwd_kernel(S, kind, last, idx, n2, mid, *refs):
    gp=refs[:8]
    out, h_ref, wd_ref, gu_s, d_s, acc, sem = refs[8:]
    j=pl.program_id(0); i=pl.program_id(1)
    @pl.when((j==0)&(i==0))
    def _():
        load_rows(idx,kind,gp,gu_s,sem.at[0])
        load_cols(idx,kind,gp,d_s,sem.at[1])
    @pl.when(i==0)
    def _():
        wait_rows(gu_s,sem.at[0],j); wait_cols(d_s,sem.at[1],j)
        for k in range(4): gu_s[4*j+k,960:1024,:]=jnp.zeros((64,2*S),BF)
        for b in range(2):
            wd_ref[0,b*2*S:(b+1)*2*S,:]=jnp.concatenate([d_s[2*j+b,k][:,:120] for k in range(8)]+[jnp.zeros((2*S,64),BF)],axis=-1)
    rows=pl.ds(pl.multiple_of(i*256,256),256)
    xb=n2[rows,:]
    acts=[]
    for q in range(2):
        w=jnp.concatenate([gu_s[4*j+2*q],gu_s[4*j+2*q+1]],axis=-1)
        h=dot(xb,w)
        h_ref[0,:,q*4*S:(q+1)*4*S]=h.astype(BF)
        for b in range(2):
            g=h[:,b*2*S:b*2*S+S]; u=h[:,b*2*S+S:b*2*S+2*S]
            acts.append((g/(1+jnp.exp(-g))*u).astype(BF))
    act=jnp.concatenate(acts,axis=-1)
    o=dot(act,wd_ref[0])
    @pl.when(j==0)
    def _(): acc[rows,:]=o+mid[rows,:]
    @pl.when(j==1)
    def _():
        r=acc[rows,:]+o
        if last: out[0,0]=r.T[:D,:].astype(BF)
        else: out[...]=r

def ffn_fwd(idx, n2, mid, gp, kind, last):
    S=gp[0].shape[2]//2
    full=pl.BlockSpec((T,DP),lambda j,i,idx:(0,0))
    if last: ospec=pl.BlockSpec((1,1,D,256),lambda j,i,idx:(flip((i*j)%2,idx[3]),flip((i*j)//2,idx[2]),0,0))
    else: ospec=pl.BlockSpec((256,DP),lambda j,i,idx:(i*j,0))
    return pl.pallas_call(functools.partial(ffn_fwd_kernel,S,kind,last), grid_spec=pltpu.PrefetchScalarGridSpec(num_scalar_prefetch=1,grid=(2,4),
        in_specs=[full,full]+[ANY]*8,
        out_specs=[ospec, pl.BlockSpec((1,256,8*S),lambda j,i,idx:(j,i,0)), pl.BlockSpec((1,4*S,DP),lambda j,i,idx:(j,0,0))],
        scratch_shapes=[pltpu.VMEM((8,DP,2*S),BF),pltpu.VMEM((4,8,2*S,128),BF),pltpu.VMEM((T,DP),F32),pltpu.SemaphoreType.DMA((2,2))]),
        out_shape=[sds((2,2,D,256),BF) if last else sds((T,DP),F32),sds((2,T,8*S),BF),sds((2,4*S,DP),BF)],
        compiler_params=params(60), cost_estimate=cost(20), name="ffn_fwd")(idx,n2,mid,*gp)

def slot_of(idx, dpi, ctx):
    z=dpi//2; x=dpi%2; y=ctx//2; c=ctx%2
    return flip(c,idx[3]), flip(x,idx[1]), flip(y,idx[2]), lax.rem(z-idx[0]+4,4)

def put(idx, src, keep, send, sem, dpi, ctx, *at):
    c,x,y,z=slot_of(idx,dpi,ctx)
    @pl.when(c==0)
    def _(): pltpu.make_async_copy(src,keep.at[(x,y,z)+at],sem).start()
    @pl.when(c==1)
    def _(): pltpu.make_async_copy(src,send.at[(x,y,z)+at],sem).start()

def ffn_bwd_kernel(S, kind, first, idx, cb, h, wd, n2h, *refs):
    if not first:
        dn2in,*refs=refs
    gp=refs[:8]
    dn2, gk, gs, n2, gu_s, dh_s, act_s, dw_s, dd_s, sem, osem, nsem = refs[8:]
    q=pl.program_id(0)
    nq=4*S
    @pl.when(q==0)
    def _():
        load_rows(idx,kind,gp,gu_s,sem)
        if not first: pltpu.make_async_copy(dn2in,dn2,nsem.at[1]).start()
        pltpu.make_async_copy(n2h,n2,nsem.at[0]).start()
    wdq=wd[0]
    def grads(i):
        rows=slice(i*256,(i+1)*256)
        dact=dot(cb[rows,:],wdq,NT)
        parts=[];acts=[]
        for b in range(4):
            g=h[0,rows,b*2*S:b*2*S+S].astype(F32); u=h[0,rows,b*2*S+S:b*2*S+2*S].astype(F32)
            da=dact[:,b*S:(b+1)*S]
            sg=1/(1+jnp.exp(-g)); sl=g*sg
            acts.append((sl*u).astype(BF))
            parts.append((da*u*(sg+sl*(1-sg))).astype(BF)); parts.append((da*sl).astype(BF))
        dh_s[rows,:]=jnp.concatenate(parts,axis=-1); act_s[rows,:]=jnp.concatenate(acts,axis=-1)
    def back(i):
        rows=slice(i*256,(i+1)*256)
        t=dot(dh_s[rows,:],w,NT)
        dn2[rows,:]=(jnp.where(q==0,0.0,dn2[rows,:]) if first else dn2[rows,:])+t
    grads(0)
    wait_rows(gu_s,sem,q)
    @pl.when(q==0)
    def _():
        if not first: pltpu.make_async_copy(dn2in,dn2,nsem.at[1]).wait()
        pltpu.make_async_copy(n2h,n2,nsem.at[0]).wait()
    @pl.when(q==1)
    def _():
        pltpu.make_async_copy(dw_s.at[pl.ds(0,960)],dw_s.at[pl.ds(0,960)],osem.at[0]).wait()
        pltpu.make_async_copy(dd_s,dd_s,osem.at[1]).wait()
    for k in range(4): gu_s[4*q+k,960:1024,:]=jnp.zeros((64,2*S),BF)
    w=jnp.concatenate([gu_s[4*q+k] for k in range(4)],axis=-1)
    for i in range(1,4):
        back(i-1)
        grads(i)
    back(3)
    for m in range(nq//256):
        r=dot(act_s[:,m*256:(m+1)*256],cb[...],TN)
        for k in range(8):
            dd_s[k,m*256:(m+1)*256,:]=jnp.concatenate([r[:,k*120:(k+1)*120],jnp.zeros((256,8),F32)],axis=-1).astype(BF)
    for k in range(8):
        for cc in range(2):
            for t in range(2*S//128):
                put(idx,dd_s.at[k,pl.ds(cc*2*S+128*t,128)],gk,gs,osem.at[1],k,2*q+cc,pl.ds(240,128),pl.ds(128*t,128))
    def dw_step(m):
        cols=pl.ds(pl.multiple_of(m*256,256),256)
        dw_s[cols,:]=dot(n2[:,cols],dh_s[...],TN).astype(BF)
        return 0
    for m in range(4): dw_step(m)
    for b in range(4):
        for ctx in range(4):
            put(idx,dw_s.at[pl.ds(ctx*240,240),pl.ds(b*2*S,2*S)],gk,gs,osem.at[0],4*q+b,ctx,pl.ds(0,240))
    @pl.when(q==1)
    def _():
        pltpu.make_async_copy(dw_s.at[pl.ds(0,960)],dw_s.at[pl.ds(0,960)],osem.at[0]).wait()
        pltpu.make_async_copy(dd_s,dd_s,osem.at[1]).wait()

def ffn_bwd(idx, cb, n2, h, wd, dn2in, gp, kind, rows):
    S=gp[0].shape[2]//2
    full=const((T,DP))
    return pl.pallas_call(functools.partial(ffn_bwd_kernel,S,kind,dn2in is None), grid=(2,),
        in_specs=[SMEM,full,pl.BlockSpec((1,T,8*S),lambda q:(q,0,0)),pl.BlockSpec((1,4*S,DP),lambda q:(q,0,0))]+[ANY]*(9+(dn2in is not None)),
        out_specs=[full,ANY,ANY],
        out_shape=[sds((T,DP),F32)]+[sds((2,2,4,rows,2*S),BF)]*2,
        scratch_shapes=[pltpu.VMEM((T,DP),BF),pltpu.VMEM((8,DP,2*S),BF),pltpu.VMEM((T,8*S),BF),pltpu.VMEM((T,4*S),BF),pltpu.VMEM((DP,8*S),BF),pltpu.VMEM((8,4*S,128),BF)]+[pltpu.SemaphoreType.DMA((2,))]*3,
        compiler_params=params(60), cost_estimate=cost(33), name="ffn_bwd")(idx,cb,h,wd,n2,*([] if dn2in is None else [dn2in]),*gp)

def block(f): return f.astype(F32)
def reduce_one_kernel(keep, rc, sx, sy, sxy):
    def s(x,y): return (block(keep[x,y,0])+block(rc[x,y,0])).astype(BF)
    sx[0]=s(1,0); sy[0]=s(0,1); sxy[0]=s(1,1)
def reduce_one(keep, rc):
    _,_,_,r,n=keep.shape
    b=pl.BlockSpec((2,2,1,r,n),lambda k:(0,0,k,0,0)); o=pl.BlockSpec((1,r,n),lambda k:(k,0,0))
    return pl.pallas_call(reduce_one_kernel,grid=(4,),in_specs=[b,b],out_specs=[o]*3,out_shape=[sds((4,r,n),BF)]*3,compiler_params=params(18),cost_estimate=cost(3),name="reduce_one")(keep,rc)
def reduce_two_kernel(keep, rc, a, b, c, own, s1, s2, s3):
    k=pl.program_id(0)
    t=block(keep[0,0,0])+block(rc[0,0,0])+block(a[0])+block(b[0])+block(c[0])
    @pl.when(k==0)
    def _(): own[...]=t
    for j,s in ((1,s1),(2,s2),(3,s3)):
        @pl.when(k==j)
        def _(s=s): s[...]=t.astype(BF)
def reduce_two(keep, rc, a, b, c):
    _,_,_,r,n=keep.shape
    kb=pl.BlockSpec((1,1,1,r,n),lambda k:(0,0,k,0,0)); ib=pl.BlockSpec((1,r,n),lambda k:(k,0,0)); ob=pl.BlockSpec((r,n),lambda k:(0,0))
    return pl.pallas_call(reduce_two_kernel,grid=(4,),in_specs=[kb,kb,ib,ib,ib],out_specs=[ob]*4,out_shape=[sds((r,n),F32)]+[sds((r,n),BF)]*3,compiler_params=params(12),cost_estimate=cost(3),name="reduce_two")(keep,rc,a,b,c)

NEG=-1e30
QB=256
def causal(keys, shape):
    a=lax.broadcasted_iota(jnp.int32,shape,keys); b=lax.broadcasted_iota(jnp.int32,shape,1-keys)%QB
    return a<=b

def attn_fwd_kernel(q, k, v, o, lse):
    n=3*QB
    for qi in range(T//QB):
        rows=slice(qi*QB,(qi+1)*QB); kn=(qi+1)*QB
        s=dot(q[:,rows,:].reshape(n,128),k[0,0:kn,:],NT)
        sd=jnp.where(causal(1,(n,QB)),s[:,kn-QB:],NEG)
        s=sd if qi==0 else jnp.concatenate([s[:,:kn-QB],sd],axis=-1)
        m=jnp.max(s,axis=-1,keepdims=True)
        r=dot(jnp.exp(s-m).astype(BF),v[0,0:kn,:])
        l=r[:,64:65]
        o[:,rows,:]=(r/l).astype(BF).reshape(3,QB,128)
        e=jnp.broadcast_to(m+jnp.log(l),(n,128)).T[0:1,:]
        for h in range(3): lse[h,:,rows]=e[:,h*QB:(h+1)*QB]

def attn_fwd(q,k,v,g0,ng):
    qs=pl.BlockSpec((3,T,128),lambda g:(g+g0,0,0)); ks=pl.BlockSpec((1,T,128),lambda g:(g+g0,0,0))
    return pl.pallas_call(attn_fwd_kernel,grid=(ng,),in_specs=[qs,ks,ks],
        out_specs=[pl.BlockSpec((3,T,128),lambda g:(g,0,0)),pl.BlockSpec((3,1,T),lambda g:(g,0,0))],
        out_shape=[sds((3*ng,T,128),BF),sds((3*ng,1,T),F32)],compiler_params=params(60),cost_estimate=cost(6*ng),name="attn_fwd")(q,k,v)

def unrot(g,c,s,low):
    t=jnp.where(low,pltpu.roll(g,96,1),-pltpu.roll(g,32,1))
    return g*c+t*s

def attn_bwd_kernel(q,k,v,do,lse,delta,c,s,dq,dk,dv,dka,dva):
    n=3*QB
    low=lax.broadcasted_iota(jnp.int32,(QB,128),1)%64<32
    nb=T//QB
    for qi in range(nb-1,-1,-1):
        rows=slice(qi*QB,(qi+1)*QB); kn=(qi+1)*QB
        qb=q[:,rows,:].reshape(n,128); dob=do[:,rows,:].reshape(n,128); kb=k[0,0:kn,:]
        cat=lambda r: jnp.concatenate([r[h,:,rows] for h in range(3)],axis=-1)
        pt=jnp.exp(dot(kb,qb,NT)-cat(lse))
        pd=jnp.where(causal(0,(QB,n)),pt[kn-QB:],0.0)
        pt=pd if qi==0 else jnp.concatenate([pt[:kn-QB],pd],axis=0)
        dst=(pt*(dot(v[0,0:kn,:],dob,NT)-cat(delta))).astype(BF)
        a=dot(pt.astype(BF),dob); b=dot(dst,qb)
        if qi==nb-1: dva[...]=a; dka[...]=b
        else: dva[0:kn,:]+=a; dka[0:kn,:]+=b
        g=dot(dst,kb,TN)*0.125
        for h in range(3):
            dq[h,rows,:]=unrot(g[h*QB:(h+1)*QB],c[rows,:],s[rows,:],low).astype(BF)
    for qi in range(nb):
        rows=slice(qi*QB,(qi+1)*QB)
        dk[0,rows,:]=unrot(dka[rows,:],c[rows,:],s[rows,:],low).astype(BF)
        dv[0,rows,:]=dva[rows,:].astype(BF)

def attn_bwd(q,k,v,do,lse,delta,c,s,g0,ng):
    qs=pl.BlockSpec((3,T,128),lambda g:(g+g0,0,0)); ks=pl.BlockSpec((1,T,128),lambda g:(g+g0,0,0))
    qo=pl.BlockSpec((3,T,128),lambda g:(g,0,0)); ko=pl.BlockSpec((1,T,128),lambda g:(g,0,0))
    return pl.pallas_call(attn_bwd_kernel,grid=(ng,),in_specs=[qs,ks,ks,qs]+[pl.BlockSpec((3,1,T),lambda g:(g+g0,0,0))]*2+[const((T,128)),const((T,128))],
        out_specs=[qo,ko,ko],
        out_shape=[sds((3*ng,T,128),BF),sds((ng,T,128),BF),sds((ng,T,128),BF)],
        scratch_shapes=[pltpu.VMEM((T,128),F32),pltpu.VMEM((T,128),F32)],
        compiler_params=params(30),cost_estimate=cost(9*ng),name="attn_bwd")(q,k,v,do,lse,delta,c,s)

EPS=1e-5
WN=1664
def prefetch(grid,in_specs,out_specs,scratch): return pltpu.PrefetchScalarGridSpec(num_scalar_prefetch=1,grid=grid,in_specs=in_specs,out_specs=out_specs,scratch_shapes=scratch)
def tok(i,idx): return (flip(i%2,idx[3]),flip(i//2,idx[2]),0,0)
tok_spec=lambda: pl.BlockSpec((1,1,D,256),tok)
row_spec=lambda n: pl.BlockSpec((256,n),lambda i,idx:(i,0))
head_spec=lambda h: pl.BlockSpec((h,256,128),lambda i,idx:(0,i,0))
def cst(shape): return pl.BlockSpec(shape,lambda *g:(0,)*len(shape))
def zeros(r,n,dt=F32): return jnp.zeros((r,n),dt)

def qkv_kernel(idx, x, c, s, *refs):
    pc=refs[:8]
    n1,q,k,v,w,gains,s1,sem=refs[8:]
    i=pl.program_id(0)
    @pl.when(i==0)
    def _():
        for src,dpi,ctx,_,_ in places(idx,"z",pc):
            pltpu.make_async_copy(src, s1.at[dpi,ctx], sem).start()
        pltpu.make_async_copy(s1,s1,sem).wait()
        for t in range(4):
            rows=slice(240*t,240*t+240)
            w[rows,:]=jnp.concatenate([s1[d,t,0:240,0:120] for d in range(8)]+[s1[d,t,0:240,128:168] for d in range(8)]+[s1[d,t,0:240,168:208] for d in range(8)]+[zeros(240,64,BF)],axis=-1)
        w[960:1024,:]=zeros(64,WN,BF)
        gl=[s1[d,t,240:256,0:128].astype(F32)[0:1,0:60] for d in range(8) for t in range(4)]
        gains[0:1,:]=jnp.concatenate(gl[:16]+[zeros(1,64)],axis=-1)
        gains[1:2,:]=jnp.concatenate(gl[16:]+[zeros(1,64)],axis=-1)
    xf=x[:,0:D].astype(F32)
    r=lax.rsqrt(jnp.sum(xf*xf,axis=-1,keepdims=True)*(1.0/D)+EPS)
    n=jnp.concatenate([(xf*r*gains[0:1,0:D]).astype(BF),zeros(256,64,BF)],axis=-1)
    n1[...]=n
    h=dot(n,w[...])
    low=lax.broadcasted_iota(jnp.int32,(256,128),1)%64<32
    z64=zeros(256,64,BF)
    one=jnp.where(lax.broadcasted_iota(jnp.int32,(256,64),1)==0,1.0,0.0).astype(BF)
    for t in range(10):
        g=h[:,128*t:128*t+128]
        u=jnp.where(low,-pltpu.roll(g,96,1),pltpu.roll(g,32,1))
        o=g*c[...]+u*s[...]
        for e in range(2):
            hd=2*t+e
            oh=o[:,64*e:64*e+64]
            if hd<15: q[hd]=jnp.concatenate([(oh*0.125).astype(BF),z64],axis=-1)
            else: k[hd-15]=jnp.concatenate([oh.astype(BF),z64],axis=-1)
    for e in range(5):
        v[e]=jnp.concatenate([h[:,1280+64*e:1344+64*e].astype(BF),one],axis=-1)

def qkv_fwd(idx,x,c,s,pc):
    return pl.pallas_call(qkv_kernel,grid_spec=prefetch((4,),[row_spec(DP),row_spec(128),row_spec(128)]+[ANY]*8,
        [row_spec(DP),head_spec(15),head_spec(5),head_spec(5),cst((DP,WN)),cst((2,DP))],
        [pltpu.VMEM((8,4,256,256),BF),pltpu.SemaphoreType.DMA]),
        out_shape=[sds((T,DP),BF),sds((15,T,128),BF),sds((5,T,128),BF),sds((5,T,128),BF),sds((DP,WN),BF),sds((2,DP),F32)],
        compiler_params=params(60),cost_estimate=cost(16), name="qkv_fwd")(idx,x,c,s,*pc)

def out_kernel(idx,o1,o2,x,gains,*refs):
    pc=refs[:8]
    att,mid,n2,wo,ws,sem=refs[8:]
    @pl.when(pl.program_id(0)==0)
    def _():
        for src,dpi,ctx,_,_ in places(idx,"z",pc):
            for t in range(3):
                pltpu.make_async_copy(src.at[pl.ds(368,80),pl.ds(128*t,128)], ws.at[dpi,pl.ds(pl.multiple_of(ctx*240+80*t,16),80)], sem).start()
        pltpu.make_async_copy(ws,ws,sem).wait()
        wo[0:D,:]=jnp.concatenate([ws[d][:,0:120] for d in range(8)]+[zeros(D,64,BF)],axis=-1)
        wo[D:DP,:]=zeros(64,DP,BF)
    a=jnp.concatenate([o[h][:,0:64] for o in (o1,o2) for h in range(o.shape[0])]+[zeros(256,64,BF)],axis=-1)
    att[...]=a
    m=dot(a,wo[...])+x[...].astype(F32)
    mid[...]=m
    r=lax.rsqrt(jnp.sum(m*m,axis=-1,keepdims=True)*(1.0/D)+EPS)
    n2[...]=(m*r*gains[1:2,:]).astype(BF)

def out_fwd(idx,o1,o2,x,gains,pc):
    return pl.pallas_call(out_kernel,grid_spec=prefetch((4,),[head_spec(o1.shape[0]),head_spec(o2.shape[0]),row_spec(DP),cst((2,DP))]+[ANY]*8,
        [row_spec(DP)]*3+[cst((DP,DP))],[pltpu.VMEM((8,D,128),BF),pltpu.SemaphoreType.DMA]),out_shape=[sds((T,DP),BF),sds((T,DP),F32),sds((T,DP),BF),sds((DP,DP),BF)],compiler_params=params(60),cost_estimate=cost(9),name="out_fwd")(idx,o1,o2,x,gains,*pc)

def tok_in_kernel(idx,h,r,g,o):
    y=idx[2]; c=idx[3]
    for ys,cs,v in ((0,0,h[2*y+c]),(1,0,r[c]),(0,1,g[0]),(1,1,g[1])):
        b=2*flip(y,ys)+flip(c,cs)
        o[pl.ds(pl.multiple_of(256*b,256),256),:]=jnp.concatenate([v,zeros(64,256,BF)],axis=0).T
def tok_in(idx,h,r,g):
    return pl.pallas_call(tok_in_kernel,in_specs=[SMEM]+[pl.BlockSpec(memory_space=pltpu.VMEM)]*3,out_specs=pl.BlockSpec(memory_space=pltpu.VMEM),out_shape=sds((T,DP),BF),compiler_params=params(14),cost_estimate=cost(4),name="tok_in")(idx,h,r,g)

def out_bwd_kernel(idx,dn2,cb,mid,gains,wo,att,kin,sin,dmid,do,dg,ok,os_,delta,dbr_s,st,sem):
    i=pl.program_id(0)
    rows=pl.ds(pl.multiple_of(i*256,256),256)
    m=mid[...]; r=lax.rsqrt(jnp.sum(m*m,axis=-1,keepdims=True)*(1.0/D)+EPS)
    d=dn2[...]; gd=gains[1:2,:]*d
    dm=cb[...].astype(F32)+r*gd-m*(r*r*r)*(jnp.sum(gd*m,axis=-1,keepdims=True)*(1.0/D))
    dmid[...]=dm
    g=jnp.sum(d*m*r,axis=0,keepdims=True)
    dg[...]=g+jnp.where(i==0,0.0,dg[...])
    b=dm.astype(BF)
    dbr_s[rows,:]=b
    da=dot(b,wo[...],NT).astype(BF)
    z64=zeros(256,64,BF)
    for h in range(15): do[h]=jnp.concatenate([da[:,64*h:64*h+64],z64],axis=-1)
    p=da.astype(F32)*att[rows,:].astype(F32)
    hi=p.astype(BF); lo=(p-hi.astype(F32)).astype(BF)
    e=jnp.where(lax.broadcasted_iota(jnp.int32,(DP,128),0)//64==lax.broadcasted_iota(jnp.int32,(DP,128),1),1.0,0.0).astype(BF)
    de=(dot(hi,e)+dot(lo,e)).T
    for h in range(15): delta[h]=de[h:h+1,:]
    @pl.when(i==3)
    def _():
        for mm in range(4):
            rr=dot(att[:,256*mm:256*mm+256],dbr_s[...],TN)
            for k in range(8):
                st[k,256*mm:256*mm+256,:]=jnp.concatenate([rr[:,120*k:120*k+120],zeros(256,8)],axis=-1).astype(BF)
        for k in range(8):
            for t in range(4):
                put(idx,st.at[k,pl.ds(240*t,128)],ok,os_,sem,k,t,pl.ds(368,128),pl.ds(0,128)); put(idx,st.at[k,pl.ds(240*t+128,112)],ok,os_,sem,k,t,pl.ds(368,112),pl.ds(128,128))
        pltpu.make_async_copy(st.at[:,pl.ds(0,960)],st.at[:,pl.ds(0,960)],sem).wait()

def out_bwd(idx,dn2,cb,mid,gains,wo,att,keep,send):
    return pl.pallas_call(out_bwd_kernel,grid_spec=prefetch((4,),[row_spec(DP)]*3+[cst((2,DP)),cst((DP,DP)),cst((T,DP)),ANY,ANY],
        [row_spec(DP),head_spec(15),cst((1,DP)),ANY,ANY,pl.BlockSpec((15,1,256),lambda i,idx:(0,0,i))],[pltpu.VMEM((T,DP),BF),pltpu.VMEM((8,DP,128),BF),pltpu.SemaphoreType.DMA]),
        out_shape=[sds((T,DP),F32),sds((15,T,128),BF),sds((1,DP),F32)]+[sds(keep.shape,BF)]*2+[sds((15,1,T),F32)],input_output_aliases={7:3,8:4},
        compiler_params=params(60),cost_estimate=cost(16), name="out_bwd")(idx,dn2,cb,mid,gains,wo,att,keep,send)

def qkv_dx_kernel(idx,dq1,dk1,dv1,dq2,dk2,dv2,dq3,dk3,dv3,x,gains,dmid,w,hg,dh,dg1):
    i=pl.program_id(0)
    h=jnp.concatenate([r[h][:,0:64] for r in (dq1,dq2,dq3,dk1,dk2,dk3,dv1,dv2,dv3) for h in range(r.shape[0])]+[zeros(256,64,BF)],axis=-1)
    dh[...]=h
    d=dot(h,w[...],NT)
    xf=x[...].astype(F32)
    r=lax.rsqrt(jnp.sum(xf*xf,axis=-1,keepdims=True)*(1.0/D)+EPS)
    gd=gains[0:1,:]*d
    hh=dmid[...]+r*gd-xf*(r*r*r)*(jnp.sum(gd*xf,axis=-1,keepdims=True)*(1.0/D))
    hg[0,0]=hh.T[:D,:].astype(BF)
    g=jnp.sum(d*xf*r,axis=0,keepdims=True)
    dg1[...]=g+jnp.where(i==0,0.0,dg1[...])

def qkv_dx(idx,g1,g2,g3,x,gains,dmid,w):
    return pl.pallas_call(qkv_dx_kernel,grid_spec=prefetch((4,),[head_spec(a.shape[0]) for a in (*g1,*g2,*g3)]+[row_spec(DP),cst((2,DP)),row_spec(DP),cst((DP,WN))],
        [tok_spec(),row_spec(WN),cst((1,DP))],[]),out_shape=[sds((2,2,D,256),BF),sds((T,WN),BF),sds((1,DP),F32)],
        compiler_params=params(24),cost_estimate=cost(9),name="qkv_dx")(idx,*g1,*g2,*g3,x,gains,dmid,w)

def qkv_dw_kernel(idx,n1,dh,dg1,dg2,wk,ws,st,sg,sem):
    m=pl.program_id(0)
    r=dot(n1[...],dh[...],TN)
    rows=pl.ds(pl.multiple_of(256*m,256),256)
    for k in range(8):
        st[k,rows,:]=jnp.concatenate([r[:,120*k:120*k+120],zeros(256,8),r[:,960+40*k:1000+40*k],r[:,1280+40*k:1320+40*k],zeros(256,48)],axis=-1).astype(BF)
    @pl.when(m==3)
    def _():
        sg[...]=jnp.zeros_like(sg)
        for k in range(8):
            for t in range(4):
                o=(4*k+t)*60
                src=dg1[:,o:o+60] if k<4 else dg2[:,o-960:o-900]
                sg[k,t,:,0:128]=jnp.broadcast_to(jnp.concatenate([src,zeros(1,68)],axis=-1),(16,128)).astype(BF)
                put(idx,st.at[k,pl.ds(240*t,240)],wk,ws,sem,k,t,pl.ds(0,240))
                put(idx,sg.at[k,t],wk,ws,sem,k,t,pl.ds(240,16))
        pltpu.make_async_copy(st.at[:,pl.ds(0,960)],st.at[:,pl.ds(0,960)],sem).wait()
        pltpu.make_async_copy(sg,sg,sem).wait()

def qkv_dw(idx,n1,dh,dg1,dg2):
    return pl.pallas_call(qkv_dw_kernel,grid_spec=prefetch((4,),[pl.BlockSpec((T,256),lambda m,idx:(0,m)),cst((T,WN)),cst((1,DP)),cst((1,DP))],
        [ANY,ANY],[pltpu.VMEM((8,DP,256),BF),pltpu.VMEM((8,4,16,256),BF),pltpu.SemaphoreType.DMA]),out_shape=[sds((2,2,4,256,256),BF)]*2,
        compiler_params=params(60),cost_estimate=cost(9),name="qkv_dw")(idx,n1,dh,dg1,dg2)

def tok_out_kernel(idx,a,r,b,o):
    y=idx[2]; c=idx[3]
    o[2*y+c]=a[0,0]; o[2*y+1-c]=r[0]
    o[2*(1-y)+c]=b[0]; o[2*(1-y)+1-c]=b[1]
def tok_out(idx,a,r,b):
    v=pl.BlockSpec(memory_space=pltpu.VMEM)
    return pl.pallas_call(tok_out_kernel,grid=(1,),in_specs=[SMEM,pl.BlockSpec((1,1,D,256),lambda i:(0,0,0,0)),pl.BlockSpec((1,D,256),lambda i:(0,0,0)),v],out_specs=v,out_shape=sds((4,D,256),BF),compiler_params=params(10),cost_estimate=cost(4),name="tok_out")(idx,a,r,b)


def swap(a, axis, bit):
    n = lax.axis_size(axis)
    return lax.ppermute(a, axis, [(i, i ^ bit) for i in range(n)])

def move(a, name):
    if name == "xy":
        n = lax.axis_size("ctx")
        return lax.ppermute(a, ("dp", "ctx"), [(i, (i // n ^ 1) * n + (i % n ^ 2)) for i in range(n * lax.axis_size("dp"))])
    if name == "x": return swap(a, "dp", 1)
    if name == "y": return swap(a, "ctx", 2)
    return swap(a, "ctx", 1)

def from_z(a, k):
    return lax.ppermute(a, "dp", [(((z + k) % 4) * 2 + x, z * 2 + x) for z in range(4) for x in range(2)])

def after(a, *others):
    return lax.optimization_barrier((a,) + others)[0]

def gather_z(shard):
    return jnp.stack([shard] + [from_z(shard, k) for k in (1, 2, 3)])

def gather_rest(g):
    ps = [g] + [move(g, name) for name in ("y", "x", "xy")]
    return ps + [move(p, "c") for p in ps]

def gather_flat(shard):
    g = jnp.stack([shard] + [move(shard, name) for name in ("y", "x", "xy")])
    ps = [g] + [from_z(g, k) for k in (1, 2, 3)]
    return ps + [move(p, "c") for p in ps]

def add(*terms):
    total = terms[0].astype(F32)
    for t in terms[1:]: total = total + t.astype(F32)
    return total

def reduce_pieces(keep, send):
    rc = move(send, "c")
    parts = reduce_one(keep, rc)
    parts = [move(p, n) for p, n in zip(parts, ("x", "y", "xy"))]
    own, *rest = reduce_two(keep, rc, *parts)
    return add(own, *[from_z(p, 3 - k) for k, p in enumerate(rest)])

def exchange_in_y(idx, a):
    return move(lax.dynamic_slice_in_dim(a, 2 * (1 - idx[2]), 2, 0), "y")

def exchange_in_c(idx, a, r):
    y, c = idx[2], idx[3]
    give = jnp.concatenate([lax.dynamic_slice_in_dim(a, 2 * y + 1 - c, 1, 0), lax.dynamic_slice_in_dim(r, 1 - c, 1, 0)])
    return move(give, "c")

SPLIT = ((0, 192), (192, 320))

def fast(hidden_in, norm_gains, w_query, w_key, w_value, w_out, w_gate, w_up, w_down, cotangent):
    di, ci = lax.axis_index("dp"), lax.axis_index("ctx")
    idx = jnp.stack([di // 2, di % 2, ci // 2, ci % 2]).astype(jnp.int32)
    pz = lambda r, n: jnp.zeros((r, n), BF)
    c1 = jnp.concatenate([w_query, pz(240, 8), w_key, w_value, pz(240, 48)], axis=1)
    gain_row = jnp.pad(norm_gains.reshape(1, 60), ((0, 15), (0, 196)))
    c1 = jnp.concatenate([c1, gain_row], axis=0)
    def pack(lo, hi):
        s = hi - lo
        gu = jnp.concatenate([w_gate[:, lo:hi], w_up[:, lo:hi]], axis=1)
        d = jnp.concatenate([w_down[lo:hi], w_down[320 + lo:320 + hi]], axis=0)
        d = jnp.pad(d, ((0, 0), (0, 8)))
        d = jnp.concatenate([d[128 * t:128 * t + 128] for t in range(2 * s // 128)], axis=1)
        return jnp.concatenate([gu, d], axis=0)
    wo = jnp.pad(w_out, ((0, 0), (0, 8)))
    wo = jnp.concatenate([wo[80 * t:80 * t + 80] for t in range(3)], axis=1)
    ht, ct = jnp.swapaxes(hidden_in, 1, 2), jnp.swapaxes(cotangent, 1, 2)
    xr = exchange_in_y(idx, ht)
    g1 = gather_z(c1)
    ga = gather_z(jnp.concatenate([pack(*SPLIT[0]), wo], axis=0))
    p1 = gather_rest(g1)
    xr = after(xr, p1[1])
    xg = exchange_in_c(idx, ht, xr)
    x = tok_in(idx, ht, xr, xg)
    pa = gather_rest(ga)
    pb = gather_flat(pack(*SPLIT[1]))
    cr = exchange_in_y(idx, ct)
    cg = exchange_in_c(idx, ct, cr)
    cos, sin = rope_tables(jnp.arange(T).astype(F32), HD)
    cos, sin = jnp.tile(cos, (1, 2)), jnp.tile(sin, (1, 2))
    n1, q, k, v, w, gains = qkv_fwd(idx, x, cos, sin, p1)
    o1, lse1 = attn_fwd(q, k, v, 0, 3)
    o2, lse2 = attn_fwd(q, k, v, 3, 2)
    att, mid, n2, wo = out_fwd(idx, o1, o2, x, gains, pa)
    acc, ha, wda = ffn_fwd(idx, n2, mid, pa, "z", False)
    out, hb, wdb = ffn_fwd(idx, n2, acc, pb, "xy", True)
    cb = tok_in(idx, ct, cr, cg)
    hr = move(out[1], "c")
    hb_ = move(jnp.stack([out[0, 1], hr[1]]), "y")
    hidden_out = tok_out(idx, out, hr, hb_)
    dn2, ka, sa = ffn_bwd(idx, cb, n2, ha, wda, None, pa, "z", 368)
    dn2, kb, sb = ffn_bwd(idx, cb, n2, hb, wdb, dn2, pb, "xy", 496)
    dmid, do, dg2, kb, sb, delta = out_bwd(idx, dn2, cb, mid, gains, wo, att, kb, sb)
    lse = jnp.concatenate([lse1, lse2], axis=0)
    b1 = attn_bwd(q, k, v, do, lse, delta, cos, sin, 0, 1)
    b2 = attn_bwd(q, k, v, do, lse, delta, cos, sin, 1, 2)
    b3 = attn_bwd(q, k, v, do, lse, delta, cos, sin, 3, 2)
    hg, dh, dg1 = qkv_dx(idx, b1, b2, b3, x, gains, dmid, w)
    kq, sq = qkv_dw(idx, n1, dh, dg1, dg2)
    gr = move(hg[1], "c")
    gb_ = move(jnp.stack([hg[0, 1], gr[1]]), "y")
    hidden_grad = tok_out(idx, hg, gr, gb_)
    factor = 1.0 / math.sqrt(lax.axis_size("dp") * hidden_in.shape[0] * T)
    ra = reduce_pieces(ka, sa) * factor
    rb = reduce_pieces(kb, sb) * factor
    rq = reduce_pieces(kq, sq) * factor
    ro = jnp.concatenate([rb[368:496, :120], rb[368:480, 128:248]], axis=0)
    gate, up, down = [], [], []
    for (lo, hi), r in zip(SPLIT, (ra, rb)):
        s = hi - lo
        gate.append(r[:240, :s]); up.append(r[:240, s:])
        d = jnp.concatenate([r[240:368, 128 * t:128 * t + 128] for t in range(2 * s // 128)], axis=0)[:, :120]
        down.append((d[:s], d[s:]))
    return (jnp.swapaxes(hidden_out, 1, 2), jnp.swapaxes(hidden_grad, 1, 2), rq[240, :60], rq[:240, :120], rq[:240, 128:168],
            rq[:240, 168:208], ro, jnp.concatenate(gate, axis=1), jnp.concatenate(up, axis=1),
            jnp.concatenate([down[0][0], down[1][0], down[0][1], down[1][1]], axis=0))


def body(hidden_in, *rest):
    seqs_here, seg_len, _ = hidden_in.shape
    if (lax.axis_size("dp"), lax.axis_size("ctx"), seqs_here, seg_len) == (8, 4, 4, 256):
        return fast(hidden_in, *rest)
    return local(hidden_in, *rest)


def solution(mesh):
    in_specs = (
        P("dp", "ctx", None),
        P(("dp", "ctx")),
        P("ctx", "dp"),
        P("ctx", "dp"),
        P("ctx", "dp"),
        P("ctx", "dp"),
        P("ctx", "dp"),
        P("ctx", "dp"),
        P("ctx", "dp"),
        P("dp", "ctx", None),
    )
    out_specs = (
        P("dp", "ctx", None),
        P("dp", "ctx", None),
        P(("dp", "ctx")),
        P("ctx", "dp"),
        P("ctx", "dp"),
        P("ctx", "dp"),
        P("ctx", "dp"),
        P("ctx", "dp"),
        P("ctx", "dp"),
        P("ctx", "dp"),
    )
    return jax.shard_map(body, mesh=mesh, in_specs=in_specs, out_specs=out_specs, check_vma=False)
```
